32 devices in a mesh: energy: 8 (over z, core), layer: 4 (over y, x).
Axes of the slice: x: 2, y: 2, z: 4, core: 2. Of those that a mesh axis runs over, the one named last changes fastest.
Arguments:
- green_blocks: bfloat16 [8, 12, 12, 1536], P('energy', None, None, 'layer'), as said below
- coupling: bfloat16 [12, 12, 4, 1536], P(None, None, None, 'layer'), may hold values from -1.75 to 1.75
- phonon_weights: float32 [2, 48, 4, 1536], P(None, None, None, 'layer'), may hold values from 0.001 to 0.01
- neighbours: int32 [4, 1536], P(None, 'layer'), may hold values from 0 to 1151, as said below
- phonon_shifts: int32 [48], replicated, may hold values from 1 to 2
Outputs:
- corrected: bfloat16 [8, 12, 12, 1536], P('energy', None, None, 'layer')
- polarization: float32 [48, 4, 1536], P(None, None, ('layer', 'energy'))
The draws below stay inside these ranges and needn't reach their ends.
Inputs may be any that keep to these rules, and one draw needn't show every extreme that they name: Every 12 x 12 block green_blocks[E, :, :, a] is symmetric. neighbours[k, a] is a place in the window of atom a: places 0 to 383 are the previous layer block, then the own block, then the next one. Slot 0 lies in the previous block, slot 1 in the next block, the other slots in the own block and never name the atom itself.
All inputs are finite; a program needn't handle non-finite values.
Results may differ from the reference program's by a relative error of at most 0.0062.
Values may be sent and summed in bfloat16 or wider, within the bound.
A program may use at most 128 MiB of HBM per device.

```python
import math
import jax
import jax.numpy as jnp
from jax import lax

NO = 12
NBR = 4
NW = 48
ATOM_DEV = 384
NE = 8
ATOMS = 1536
N_LAYER = 4


def draw_green_blocks(key, part):
    values = jax.random.truncated_normal(key, -3.0, 3.0, (NE, NO, NO, ATOMS), jnp.float32)
    symmetric = (values + jnp.swapaxes(values, 1, 2)) * 0.70710678
    return symmetric.astype(jnp.bfloat16)


def draw_neighbours(key, part):
    keys = jax.random.split(jax.random.fold_in(key, 11), 3)
    before = jax.random.randint(keys[0], (1, ATOMS), 0, ATOM_DEV, dtype=jnp.int32)
    after = jax.random.randint(keys[1], (1, ATOMS), 2 * ATOM_DEV, 3 * ATOM_DEV, dtype=jnp.int32)
    offsets = jax.random.randint(keys[2], (NBR - 2, ATOMS), 1, ATOM_DEV, dtype=jnp.int32)
    places = jnp.arange(ATOMS, dtype=jnp.int32) % ATOM_DEV
    inside = ATOM_DEV + (places[None, :] + offsets) % ATOM_DEV
    result = jnp.concatenate([before, after, inside], axis=0)
    result = result.at[0, 0].set(0)
    result = result.at[1, ATOMS - 1].set(3 * ATOM_DEV - 1)
    return result


def draw_phonon_shifts(key, part):
    largest = NE // 4
    values = jax.random.randint(jax.random.fold_in(key, 23), (NW,), 1, largest + 1, dtype=jnp.int32)
    values = values.at[0].set(1)
    values = values.at[1].set(largest)
    return values


def levels(key, extent, shards, low, top_value):
    gain, own = 1.0, jax.random.fold_in(key, 6)
    for dim, parts in shards:
        draws = jnp.exp(jax.random.uniform(jax.random.fold_in(own, dim), (parts,), jnp.float32, low / len(shards), top_value / len(shards)))
        gain = gain * jnp.repeat(draws, extent[dim] // parts).reshape([-1 if axis == dim else 1 for axis in range(len(extent))])
    return gain


def noise(stream_key, dims, spread, most, cuts=(), kind=jnp.bfloat16):
    array = spread * jax.random.normal(stream_key, dims, jnp.float32)
    if cuts:
        array = array * levels(stream_key, dims, cuts, -0.22, 0.18)
    return jnp.clip(array, -most, most).astype(kind)


def setup_inputs(seed: int = 0) -> dict:
    key_of = jax.random.split(jax.random.key(seed), 6)
    return {
        "green_blocks": draw_green_blocks(jax.random.fold_in(key_of[5], 71), 0),
        "coupling": noise(key_of[1], (NO, NO, NBR, ATOMS), NO ** -0.5, 1.75, ((3, 4),)),
        "phonon_weights": jnp.clip(jnp.exp(math.log(0.01) - 2.30258502 * jax.random.uniform(key_of[2], (2, NW, NBR, ATOMS), jnp.float32) ** levels(key_of[2], (2, NW, NBR, ATOMS), ((3, 4),), -0.2, 0.2)), 0.001, 0.01),
        "neighbours": draw_neighbours(jax.random.fold_in(key_of[5], 71), 0),
        "phonon_shifts": draw_phonon_shifts(jax.random.fold_in(key_of[5], 71), 0),
    }


def shift_tables(phonon_shifts, energy_count):
    energies = jnp.arange(energy_count, dtype=jnp.int32)
    target = energies[None, :, None]
    source = energies[None, None, :]
    offsets = phonon_shifts[:, None, None]
    lower_table = (source == target - offsets).astype(jnp.float32)
    upper_table = (source == target + offsets).astype(jnp.float32)
    return (lower_table, upper_table)

def reference(green_blocks, coupling, phonon_weights, neighbours, phonon_shifts):
    highest = lax.Precision.HIGHEST
    lower_table, upper_table = shift_tables(phonon_shifts, NE)
    padded = jnp.pad(green_blocks, ((0, 0), (0, 0), (0, 0), (ATOM_DEV, ATOM_DEV)))
    norm_factor = 1.0 / (NO * math.sqrt(NE))

    def one_slab(layer_index):
        atom_start = (layer_index * ATOM_DEV).astype(jnp.int32)
        window = lax.dynamic_slice_in_dim(padded, atom_start, 3 * ATOM_DEV, 3)
        slab_green = lax.dynamic_slice_in_dim(green_blocks, atom_start, ATOM_DEV, 3).astype(jnp.float32)
        slab_coupling = lax.dynamic_slice_in_dim(coupling, atom_start, ATOM_DEV, 3).astype(jnp.float32)
        slab_weights = lax.dynamic_slice_in_dim(phonon_weights, atom_start, ATOM_DEV, 3)
        slab_neighbours = lax.dynamic_slice_in_dim(neighbours, atom_start, ATOM_DEV, 1)
        gathered = jnp.take(window, slab_neighbours, axis=3).astype(jnp.float32)
        first_product = jnp.einsum('ipka,epqka->eiqka', slab_coupling, gathered, precision=highest)
        product = jnp.einsum('eiqka,jqka->eijka', first_product, slab_coupling, precision=highest).astype(jnp.bfloat16)
        product_wide = product.astype(jnp.float32)
        kernel = jnp.einsum('wka,wef->akef', slab_weights[0], lower_table, precision=highest)
        kernel = kernel + jnp.einsum('wka,wef->akef', slab_weights[1], upper_table, precision=highest)
        self_energy = jnp.einsum('akef,fijka->eija', kernel, product_wide, precision=highest).astype(jnp.bfloat16)
        correlation = jnp.einsum('fijka,eija->akfe', product_wide, slab_green, precision=highest)
        polarization = jnp.einsum('wef,akfe->wka', upper_table, correlation, precision=highest) * norm_factor
        left_product = jnp.einsum('eipa,epja->eija', slab_green, self_energy.astype(jnp.float32), precision=highest).astype(jnp.bfloat16)
        corrected = slab_green + jnp.einsum('eipa,epja->eija', left_product.astype(jnp.float32), slab_green, precision=highest)
        return (corrected.astype(jnp.bfloat16), polarization)
    corrected, polarization = lax.map(one_slab, jnp.arange(N_LAYER, dtype=jnp.int32))
    corrected = jnp.moveaxis(corrected, 0, 3).reshape(NE, NO, NO, ATOMS)
    polarization = jnp.moveaxis(polarization, 0, 2).reshape(NW, NBR, ATOMS)
    return (corrected, polarization)
```

```python
import functools
import math

import jax
import jax.numpy as jnp
import numpy as np
from jax import lax
from jax.experimental import pallas as pl
from jax.experimental.pallas import tpu as pltpu
from jax.sharding import PartitionSpec as P

MESH = pl.DeviceIdType.MESH
LANES = 128
F32 = jnp.float32
BF16 = jnp.bfloat16
VMEM_LIMIT = 48 * 1024 * 1024


def offsets(order):
    return [p * order - p * (p - 1) // 2 for p in range(order)]


def segments(order, packed):
    plan, start, first = [], 0, 0
    for i in range(0, order, 2):
        done = sum(order - n for n in range(i + 2))
        stop = packed if i + 2 >= order else done // 16 * 16
        if stop - start >= 32 or stop == packed:
            plan.append((start, stop, first, i + 2))
            start, first = stop, i + 2
    return plan


def expansion(order, row_stride, packed_rows):
    off = offsets(order)
    table = np.zeros((order * row_stride, packed_rows), np.float32)
    for p in range(order):
        for q in range(order):
            low, high = min(p, q), max(p, q)
            table[p * row_stride + q, off[low] + high - low] = 1.0
    return jnp.asarray(table, BF16)


def kernel(
    reach, shift_hbm, green_hbm, coup_hbm, weight_hbm, near_hbm, e12_hbm,
    e16_hbm, cor_ref, pol_ref,
    shift_ref, green_ref, coup_ref, weight_ref, near_ref, e12_ref, e16_ref, sig_ref,
    g16, s16, l16, tri32, own, halo, gin, pout, pin, pacc, hots, chunks, cin, c4, g3, pscr, ab,
    load_sem, hop_sem, halo_send, halo_recv, gin_send, gin_recv, part_send, part_recv,
    chunk_send, chunk_recv,
):
    order = green_ref.shape[0]
    atoms = green_ref.shape[2]
    nbr = near_ref.shape[0]
    freqs = shift_ref.shape[0]
    tiles = atoms // LANES
    packed = own.shape[0]
    pad = c4.shape[3]
    ne = lax.axis_size("energy")
    nl = lax.axis_size("layer")
    me = lax.axis_index("energy")
    layer = lax.axis_index("layer")
    share = atoms // ne
    off = offsets(order)
    plan = segments(order, packed)
    groups = (tuple(range(2, nbr)), (0, 1))

    def load(n, src, dst):
        copy = pltpu.make_async_copy(src, dst, load_sem.at[n])
        copy.start()
        return copy

    load_green = load(0, green_hbm, green_ref)
    load_near = load(1, near_hbm, near_ref)
    load_e12 = load(2, e12_hbm, e12_ref)
    load_coup = load(3, coup_hbm, coup_ref)
    load_weight = load(4, weight_hbm, weight_ref)
    load_shift = load(5, shift_hbm, shift_ref)
    load_e16 = load(6, e16_hbm, e16_ref)

    barrier = pltpu.get_barrier_semaphore()

    def greet(sem, energy, row):
        pl.semaphore_signal(
            sem, inc=1, device_id={"energy": energy, "layer": row}, device_id_type=MESH
        )

    def greet_near(sem):
        for d in range(1, reach + 1):

            @pl.when(me + d < ne)
            def _():
                greet(sem, me + d, layer)

            @pl.when(me >= d)
            def _():
                greet(sem, me - d, layer)

    near_count = jnp.minimum(me, reach) + jnp.minimum(ne - 1 - me, reach)
    rounds = -(-(ne - 1) // reach) - 1
    passed = []

    def pass_on():
        n = len(passed)
        if n < rounds:
            pl.semaphore_wait(hop_sem.at[n], near_count)
            if n + 1 < rounds:
                greet_near(hop_sem.at[n + 1])
            passed.append(n)

    greet_near(barrier)

    @pl.when(layer > 0)
    def _():
        pl.semaphore_signal(
            barrier, inc=1, device_id={"energy": me, "layer": layer - 1}, device_id_type=MESH
        )

    @pl.when(layer < nl - 1)
    def _():
        pl.semaphore_signal(
            barrier, inc=1, device_id={"energy": me, "layer": layer + 1}, device_id_type=MESH
        )

    tri32[...] = jnp.zeros_like(tri32)
    load_green.wait()
    for p in range(order):
        tri32[off[p] : off[p] + order - p, :] = green_ref[p].astype(F32)[p:, :]
    own[...] = tri32[...].astype(BF16)

    @pl.when(layer == 0)
    def _():
        halo[0] = jnp.zeros((packed, atoms), BF16)

    @pl.when(layer == nl - 1)
    def _():
        halo[1] = jnp.zeros((packed, atoms), BF16)

    for d in range(1, reach + 1):

        @pl.when(me < d)
        def _():
            gin[d - 1] = jnp.zeros((packed, atoms), BF16)
            pin[2 * d - 2] = jnp.zeros(pin.shape[1:], BF16)

        @pl.when(me + d >= ne)
        def _():
            pin[2 * d - 1] = jnp.zeros(pin.shape[1:], BF16)

    pl.semaphore_wait(
        barrier, near_count + (layer > 0).astype(jnp.int32) + (layer < nl - 1).astype(jnp.int32)
    )

    def remote(src, dst, send, recv, energy, row):
        return pltpu.make_async_remote_copy(
            src_ref=src, dst_ref=dst, send_sem=send, recv_sem=recv,
            device_id={"energy": energy, "layer": row}, device_id_type=MESH,
        )

    def halo_copy(side):
        row = layer + 1 if side == 0 else layer - 1
        return remote(own, halo.at[side], halo_send.at[side], halo_recv.at[side], me, row)

    def green_copy(d):
        return remote(
            own, gin.at[d - 1], gin_send.at[d - 1], gin_recv.at[d - 1], me + d, layer
        )

    def part_copy(slot, n, energy):
        start, stop, _, _ = plan[n]
        rows = pl.ds(start, stop - start)
        return remote(
            pout.at[slot, rows], pin.at[slot, rows], part_send.at[slot, n],
            part_recv.at[slot, n], energy, layer,
        )

    def chunk_copy(r):
        dest = lax.rem(me + r, ne)
        return remote(
            chunks.at[dest], cin.at[r], chunk_send.at[r], chunk_recv.at[r], dest, layer
        )

    has_above, has_below = layer < nl - 1, layer > 0

    @pl.when(has_below)
    def _():
        halo_copy(1).start()

    @pl.when(has_above)
    def _():
        halo_copy(0).start()

    for d in range(1, reach + 1):

        @pl.when(me + d < ne)
        def _():
            green_copy(d).start()

    if rounds:
        greet_near(hop_sem.at[0])

    row = lax.broadcasted_iota(jnp.int32, (atoms, atoms), 0)

    def one_hot(k, start):
        return jnp.where(row == near_ref[k : k + 1, :] - start, 1.0, 0.0).astype(BF16)

    def pick_neighbours(g, j, full, hot):
        size = len(groups[g])
        found = jnp.dot(full, hot, preferred_element_type=F32)
        for t in range(tiles):
            g3[pl.ds(t * size + j, order * order, stride=pad), :] = found[
                :, t * LANES : (t + 1) * LANES
            ]

    def expanded(block):
        return jnp.dot(e12_ref[...], block, preferred_element_type=F32).astype(BF16)

    load_near.wait()
    load_e12.wait()
    own_full = expanded(own[...])
    for j in range(len(groups[0])):
        pick_neighbours(0, j, own_full, one_hot(groups[0][j], atoms))
    hots[0] = one_hot(0, 0)
    hots[1] = one_hot(1, 2 * atoms)

    load_coup.wait()
    for g, slots in enumerate(groups):
        size = len(slots)
        for t in range(tiles):
            block = coup_ref[:, :, t * LANES : (t + 1) * LANES].astype(F32)
            block = block.reshape(order, order, nbr, LANES)
            c4[g, :, :, t * size : (t + 1) * size, :] = block[
                :, :, slots[0] : slots[0] + size, :
            ]

    last = off[-1] + 1
    for g in range(2):
        pscr[g, last * pad :, :] = jnp.zeros(((packed - last) * pad, LANES), F32)

    def products(g, start, stop):
        for i in range(start, stop, 2):
            first = jnp.zeros((2, order, pad, LANES), F32)
            for p in range(order):
                block = g3[p * order * pad : (p + 1) * order * pad, :]
                block = block.reshape(order, pad, LANES)
                first = first + c4[g, i : i + 2, p][:, None] * block[None]
            total = first[:, 0][:, None] * c4[g, i:, 0][None]
            for q in range(1, order):
                total = total + first[:, q][:, None] * c4[g, i:, q][None]
            total = total.astype(BF16).astype(F32)
            for n in range(2):
                pscr[g, off[i + n] * pad : (off[i + n] + order - i - n) * pad, :] = total[
                    n, n:
                ].reshape(-1, LANES)

    products(0, 0, order)
    pass_on()

    load_weight.wait()
    load_shift.wait()

    def add_weights(w, sums):
        shift = shift_ref[w]
        low, high = weight_ref[w], weight_ref[freqs + w]
        new = []
        for d in range(1, reach + 1):
            pick = jnp.where(shift == d, 1.0, 0.0).astype(F32)
            new += [sums[2 * d - 2] + pick * low, sums[2 * d - 1] + pick * high]
        return tuple(new)

    sums = lax.fori_loop(
        0, freqs, add_weights, tuple(jnp.zeros((nbr, atoms), F32) for _ in range(2 * reach)),
        unroll=4,
    )
    for s in range(2 * reach):
        ab[s] = sums[s]

    def rows_of(g, t, j, start, stop):
        at = start * pad + t * len(groups[g]) + j
        return pscr[g, pl.ds(at, stop - start, stride=pad), :]

    def partials(g, t, s, start, stop):
        lanes = slice(t * LANES, (t + 1) * LANES)
        total = None
        for j, k in enumerate(groups[g]):
            term = ab[s, k : k + 1, lanes] * rows_of(g, t, j, start, stop)
            total = term if total is None else total + term
        return total

    for t in range(tiles):
        for s in range(2 * reach):
            pacc[s, :, t * LANES : (t + 1) * LANES] = partials(0, t, s, 0, packed)

    pass_on()
    load_e16.wait()
    g16[...] = jnp.zeros_like(g16)
    for p in range(order):
        g16[p, :order, :] = green_ref[p].astype(F32)
    while len(passed) < rounds:
        pass_on()

    @pl.when(has_below)
    def _():
        halo_copy(0).wait_recv()

    @pl.when(has_above)
    def _():
        halo_copy(1).wait_recv()

    pick_neighbours(1, 0, expanded(halo[0]), hots[0])
    pick_neighbours(1, 1, expanded(halo[1]), hots[1])
    width = chunks.shape[2]

    for n, (start, stop, first, final) in enumerate(plan):
        products(1, first, final)
        for t in range(tiles):
            lanes = slice(t * LANES, (t + 1) * LANES)
            for s in range(2 * reach):
                total = pacc[s, start:stop, lanes] + partials(1, t, s, start, stop)
                pout[s, start:stop, lanes] = total.astype(BF16)
        for d in range(1, reach + 1):

            @pl.when(me + d < ne)
            def _():
                part_copy(2 * d - 2, n, me + d).start()

            @pl.when(me >= d)
            def _():
                part_copy(2 * d - 1, n, me - d).start()

    for d in range(1, reach + 1):

        @pl.when(me >= d)
        def _():
            green_copy(d).wait_recv()

    index = lax.broadcasted_iota(jnp.int32, (packed, LANES), 0)
    twice = jnp.full((packed, LANES), 2.0, F32)
    for p in range(order):
        twice = jnp.where(index == off[p], 1.0, twice)
    rows = [[None] * tiles for _ in range(reach * nbr)]

    def correlate(g, start, stop):
        for t in range(tiles):
            lanes = slice(t * LANES, (t + 1) * LANES)
            greens = [
                gin[d, start:stop, lanes].astype(F32) * twice[start:stop] for d in range(reach)
            ]
            for j, k in enumerate(groups[g]):
                value = rows_of(g, t, j, start, stop)
                for d in range(reach):
                    term = jnp.sum(greens[d] * value, axis=0, keepdims=True)
                    old = rows[d * nbr + k][t]
                    rows[d * nbr + k][t] = term if old is None else old + term

    correlate(0, 0, packed)
    correlate(1, 0, packed)
    corr = jnp.concatenate([jnp.concatenate(r, axis=1) for r in rows], axis=0)
    for e in range(ne):
        moved = corr if e == 0 else pltpu.roll(corr, atoms - e * share, 1)
        chunks[e] = moved[:, :width]
    for r in range(1, ne):
        chunk_copy(r).start()

    for n, (start, stop, _, _) in enumerate(plan):
        for d in range(1, reach + 1):

            @pl.when(me >= d)
            def _():
                part_copy(2 * d - 2, n, me).wait_recv()

            @pl.when(me + d < ne)
            def _():
                part_copy(2 * d - 1, n, me).wait_recv()

        sigma = pin[0, start:stop].astype(F32)
        for s in range(1, 2 * reach):
            sigma = sigma + pin[s, start:stop].astype(F32)
        sig_ref[start:stop, :] = sigma.astype(BF16)

    s16[...] = jnp.dot(
        e16_ref[...], sig_ref[...], preferred_element_type=F32
    ).reshape(s16.shape)

    for i in range(0, order, 2):
        left = [g16[i + n, 0:1, :] * s16[0] for n in range(2)]
        for p in range(1, order):
            block = s16[p]
            left = [left[n] + g16[i + n, p : p + 1, :] * block for n in range(2)]
        for n in range(2):
            l16[i + n] = left[n].astype(BF16).astype(F32)
    for i in range(0, order, 2):
        total = [g16[i + n] for n in range(2)]
        for p in range(order):
            block = g16[p]
            total = [total[n] + l16[i + n, p : p + 1, :] * block for n in range(2)]
        for n in range(2):
            cor_ref[i + n] = total[n][:order].astype(BF16)

    for r in range(1, ne):
        chunk_copy(r).wait_recv()
    summed = chunks[me]
    for r in range(1, ne):
        summed = summed + cin[r]
    summed = summed[:, :share] * (1.0 / (order * math.sqrt(ne)))
    for w in range(freqs):
        shift = shift_ref[w]
        value = jnp.zeros((nbr, share), F32)
        for d in range(1, reach + 1):
            value = jnp.where(shift == d, summed[(d - 1) * nbr : d * nbr], value)
        pol_ref[w] = value

    @pl.when(has_above)
    def _():
        halo_copy(0).wait_send()

    @pl.when(has_below)
    def _():
        halo_copy(1).wait_send()

    for d in range(1, reach + 1):

        @pl.when(me + d < ne)
        def _():
            green_copy(d).wait_send()
            for n in range(len(plan)):
                part_copy(2 * d - 2, n, me).wait_send()

        @pl.when(me >= d)
        def _():
            for n in range(len(plan)):
                part_copy(2 * d - 1, n, me).wait_send()

    for r in range(1, ne):
        chunk_copy(r).wait_send()


def finish(cor_ref, pol_ref, cor_hbm, pol_hbm, sem):
    first = pltpu.make_async_copy(cor_ref, cor_hbm, sem.at[0])
    second = pltpu.make_async_copy(pol_ref, pol_hbm, sem.at[1])
    first.start()
    second.start()
    first.wait()
    second.wait()


def body(green_blocks, coupling, phonon_weights, neighbours, phonon_shifts):
    ne = lax.axis_size("energy")
    reach = max(ne // 4, 1)
    order = green_blocks.shape[1]
    atoms = green_blocks.shape[3]
    nbr = neighbours.shape[0]
    freqs = phonon_shifts.shape[0]
    tiles = atoms // LANES
    share = atoms // ne
    count = order * (order + 1) // 2
    packed = -(-count // 16) * 16
    pad = -(-(tiles * max(nbr - 2, 2)) // 8) * 8
    rows = 16 * (-(-order // 16))
    width = -(-share // LANES) * LANES
    parts = len(segments(order, packed))
    vmem = pl.BlockSpec(memory_space=pltpu.VMEM)
    hbm = pl.BlockSpec(memory_space=pltpu.HBM)
    dma = pltpu.SemaphoreType.DMA
    green = green_blocks[0]
    staged = pl.pallas_call(
        functools.partial(kernel, reach),
        out_shape=(
            jax.ShapeDtypeStruct((order, order, atoms), BF16),
            jax.ShapeDtypeStruct((freqs, nbr, share), F32),
        ),
        in_specs=[hbm] * 7,
        out_specs=(vmem, vmem),
        scratch_shapes=[
            pltpu.SMEM((freqs,), jnp.int32),
            pltpu.VMEM((order, order, atoms), BF16),
            pltpu.VMEM((order * order, nbr, atoms), BF16),
            pltpu.VMEM((2 * freqs, nbr, atoms), F32),
            pltpu.VMEM((nbr, atoms), jnp.int32),
            pltpu.VMEM((order * order, packed), BF16),
            pltpu.VMEM((order * rows, packed), BF16),
            pltpu.VMEM((packed, atoms), BF16),
            pltpu.VMEM((order, rows, atoms), F32),
            pltpu.VMEM((order, rows, atoms), F32),
            pltpu.VMEM((order, rows, atoms), F32),
            pltpu.VMEM((packed, atoms), F32),
            pltpu.VMEM((packed, atoms), BF16),
            pltpu.VMEM((2, packed, atoms), BF16),
            pltpu.VMEM((reach, packed, atoms), BF16),
            pltpu.VMEM((2 * reach, packed, atoms), BF16),
            pltpu.VMEM((2 * reach, packed, atoms), BF16),
            pltpu.VMEM((2 * reach, packed, atoms), F32),
            pltpu.VMEM((2, atoms, atoms), BF16),
            pltpu.VMEM((ne, reach * nbr, width), F32),
            pltpu.VMEM((ne, reach * nbr, width), F32),
            pltpu.VMEM((2, order, order, pad, LANES), F32),
            pltpu.VMEM((order * order * pad, LANES), F32),
            pltpu.VMEM((2, packed * pad, LANES), F32),
            pltpu.VMEM((2 * reach, nbr, atoms), F32),
            dma((7,)), pltpu.SemaphoreType.REGULAR((max(-(-(ne - 1) // reach) - 1, 1),)),
            dma((2,)), dma((2,)), dma((reach,)), dma((reach,)),
            dma((2 * reach, parts)), dma((2 * reach, parts)), dma((ne,)), dma((ne,)),
        ],
        compiler_params=pltpu.CompilerParams(
            collective_id=0, has_side_effects=True, vmem_limit_bytes=VMEM_LIMIT
        ),
    )(
        *(
            pltpu.with_memory_space_constraint(x, pltpu.HBM)
            for x in (
                phonon_shifts,
                green,
                coupling.reshape(order * order, nbr, atoms),
                phonon_weights.reshape(2 * freqs, nbr, atoms),
                neighbours,
                expansion(order, order, packed),
                expansion(order, rows, packed),
            )
        )
    )
    corrected, polarization = pl.pallas_call(
        finish,
        out_shape=(
            jax.ShapeDtypeStruct((order, order, atoms), BF16),
            jax.ShapeDtypeStruct((freqs, nbr, share), F32),
        ),
        in_specs=[vmem, vmem],
        out_specs=(hbm, hbm),
        scratch_shapes=[dma((2,))],
        compiler_params=pltpu.CompilerParams(vmem_limit_bytes=VMEM_LIMIT),
    )(*staged)
    return corrected[None], polarization


def solution(mesh):
    return jax.shard_map(
        body,
        mesh=mesh,
        in_specs=(
            P("energy", None, None, "layer"),
            P(None, None, None, "layer"),
            P(None, None, None, "layer"),
            P(None, "layer"),
            P(),
        ),
        out_specs=(P("energy", None, None, "layer"), P(None, None, ("layer", "energy"))),
        check_vma=False,
    )
```

```python
import functools
import math

import jax
import jax.numpy as jnp
from jax import lax
from jax.experimental import pallas as pl
from jax.experimental.pallas import tpu as pltpu
from jax.sharding import PartitionSpec as P

MESH = pl.DeviceIdType.MESH
LANES = 128
F32 = jnp.float32
BF16 = jnp.bfloat16
VMEM_LIMIT = 48 * 1024 * 1024


def offsets(order):
    return [p * order - p * (p - 1) // 2 for p in range(order)]


def segments(order, packed):
    off = offsets(order)
    plan, start, first = [], 0, 0
    for rows in (2, 4):
        if rows < order and off[rows] // 16 * 16 > start:
            stop = off[rows] // 16 * 16
            plan.append((start, stop, first, rows))
            start, first = stop, rows
    middle = start + (packed - start) * 2 // 3 // 16 * 16
    if middle > start:
        plan.append((start, middle, first, order))
        start, first = middle, order
    return plan + [(start, packed, first, order)]


def complete(order, stop):
    return sum(o + order - p <= stop for p, o in enumerate(offsets(order)))


def expansion(order, row_stride, packed_rows):
    row = lax.broadcasted_iota(jnp.int32, (order * row_stride, packed_rows), 0)
    column = lax.broadcasted_iota(jnp.int32, (order * row_stride, packed_rows), 1)
    p, q = row // row_stride, row % row_stride
    low, high = jnp.minimum(p, q), jnp.maximum(p, q)
    entry = low * order - low * (low - 1) // 2 + high - low
    return jnp.where((entry == column) & (q < order), 1.0, 0.0).astype(BF16)


def kernel(
    reach, shift_hbm, green_hbm, coup_hbm, weight_hbm, near_hbm, cor_ref, pol_ref,
    shift_ref, green_ref, coup_ref, weight_ref, near_ref, e16_ref, sig_ref,
    g16, s16, l16, tri32, own, halo, gin, pout, pin, pacc, hots, chunks, cin, c4, g3, g3b, pscr, ab,
    load_sem, side_sem, near_sem, far_sem, halo_send, halo_recv, gin_send, gin_recv, part_send, part_recv,
    chunk_send, chunk_recv,
):
    order = green_ref.shape[0]
    atoms = green_ref.shape[2]
    nbr = near_ref.shape[0]
    freqs = shift_ref.shape[0]
    tiles = atoms // LANES
    packed = own.shape[0]
    pad = c4.shape[3]
    ne = lax.axis_size("energy")
    nl = lax.axis_size("layer")
    me = lax.axis_index("energy")
    layer = lax.axis_index("layer")
    share = atoms // ne
    depth = s16.shape[1]
    off = offsets(order)
    plan = segments(order, packed)
    groups = (tuple(range(2, nbr)), (0, 1))

    def load(n, src, dst):
        copy = pltpu.make_async_copy(src, dst, load_sem.at[n])
        copy.start()
        return copy

    load_green = load(0, green_hbm, green_ref)
    load_near = load(1, near_hbm, near_ref)
    load_coup = load(2, coup_hbm, coup_ref)
    load_weight = load(3, weight_hbm, weight_ref)
    load_shift = load(4, shift_hbm, shift_ref)

    barrier = pltpu.get_barrier_semaphore()

    def greet(sem, energy, row):
        pl.semaphore_signal(
            sem, inc=1, device_id={"energy": energy, "layer": row}, device_id_type=MESH
        )

    odd = lax.rem(me, 2) == 1
    even = jnp.logical_not(odd)
    has_above, has_below = layer < nl - 1, layer > 0
    near_above = jnp.minimum(ne - 1 - me, reach)
    near_count = near_above + jnp.minimum(me, reach)
    far_above = ne - 1 - me - near_above

    for d in range(1, ne):

        @pl.when(me + d < ne)
        def _():
            greet(barrier, me + d, layer)

    @pl.when(has_above)
    def _():
        greet(barrier, me, layer + 1)

    @pl.when(has_below)
    def _():
        greet(barrier, me - lax.rem(me, 2) + 1, layer - 1)

    @pl.when(odd)
    def _():
        greet(barrier, me - 1, layer)

    tri32[...] = jnp.zeros_like(tri32)
    e16_ref[...] = expansion(order, depth, packed)
    load_green.wait()
    for p in range(order):
        tri32[off[p] : off[p] + order - p, :] = green_ref[p].astype(F32)[p:, :]
    own[...] = tri32[...].astype(BF16)

    @pl.when(jnp.logical_not(has_above & has_below))
    def _():
        g3b[...] = jnp.zeros_like(g3b)

    for d in range(1, reach + 1):

        @pl.when(me < d)
        def _():
            gin[d - 1] = jnp.zeros((packed, atoms), BF16)
            pin[2 * d - 2] = jnp.zeros(pin.shape[1:], BF16)

        @pl.when(me + d >= ne)
        def _():
            pin[2 * d - 1] = jnp.zeros(pin.shape[1:], BF16)

    pl.semaphore_wait(
        barrier,
        me
        + even.astype(jnp.int32)
        + has_below.astype(jnp.int32)
        + 2 * (odd & has_above).astype(jnp.int32),
    )

    def remote(src, dst, send, recv, energy, row):
        return pltpu.make_async_remote_copy(
            src_ref=src, dst_ref=dst, send_sem=send, recv_sem=recv,
            device_id={"energy": energy, "layer": row}, device_id_type=MESH,
        )

    def halo_copy(side):
        row = layer + 1 if side == 0 else layer - 1
        return remote(own, halo.at[side], halo_send.at[0], halo_recv.at[side], me, row)

    def green_copy(d):
        return remote(
            own, gin.at[d - 1], gin_send.at[0], gin_recv.at[0], me + d, layer
        )

    def part_copy(slot, n, energy):
        start, stop, _, _ = plan[n]
        rows = pl.ds(start, stop - start)
        return remote(
            pout.at[slot, rows], pin.at[slot, rows], part_send.at[0], part_recv.at[n],
            energy, layer,
        )

    def chunk_copy(r):
        dest = lax.rem(me + r, ne)
        return remote(
            chunks.at[dest], cin.at[r], chunk_send.at[0], chunk_recv.at[0], dest, layer
        )

    def wait_gin(send):
        number = jnp.minimum(ne - 1 - me, reach) if send else jnp.minimum(me, reach)
        for c in range(1, reach + 1):

            @pl.when(number == c)
            def _():
                some = gin.at[pl.ds(0, c)]
                copy = remote(some, some, gin_send.at[0], gin_recv.at[0], me, layer)
                copy.wait_send() if send else copy.wait_recv()

    def wait_parts(rows, recv, send):
        for c in range(1, 2 * reach + 1):

            @pl.when(near_count == c)
            def _():
                some = pin.at[pl.ds(0, c), rows]
                copy = remote(some, some, part_send.at[0], part_recv.at[recv], me, layer)
                copy.wait_send() if send else copy.wait_recv()

    def wait_chunks():
        some = cin.at[pl.ds(1, ne - 1)]
        return remote(some, some, chunk_send.at[0], chunk_recv.at[0], me, layer)

    @pl.when(has_below)
    def _():
        halo_copy(1).start()

    @pl.when(odd & has_above)
    def _():
        halo_copy(0).start()
        greet(side_sem, me - 1, layer)

    for d in range(1, ne):

        @pl.when(me >= d)
        def _():
            greet(near_sem if d <= reach else far_sem, me - d, layer)

    picked = (g3, g3b)
    row = lax.broadcasted_iota(jnp.int32, (atoms, atoms), 0)

    def one_hot(k, start):
        return jnp.where(row == near_ref[k : k + 1, :] - start, 1.0, 0.0).astype(BF16)

    def pick_neighbours(g, j, blocks, hot):
        size = len(groups[g])
        found = jnp.dot(blocks, hot, preferred_element_type=F32)
        for t in range(tiles):
            picked[g][pl.ds(t * size + j, packed, stride=pad), :] = found[
                :, t * LANES : (t + 1) * LANES
            ]

    load_near.wait()
    for j in range(len(groups[0])):
        pick_neighbours(0, j, own[...], one_hot(groups[0][j], atoms))
    hots[0] = one_hot(0, 0)
    hots[1] = one_hot(1, 2 * atoms)

    load_coup.wait()
    for g, slots in enumerate(groups):
        size = len(slots)
        for t in range(tiles):
            block = coup_ref[:, :, t * LANES : (t + 1) * LANES].astype(F32)
            block = block.reshape(order, order, nbr, LANES)
            c4[g, :, :, t * size : (t + 1) * size, :] = block[
                :, :, slots[0] : slots[0] + size, :
            ]

    last = off[-1] + 1
    for g in range(2):
        pscr[g, last * pad :, :] = jnp.zeros(((packed - last) * pad, LANES), F32)

    def entry(g, low, high):
        at = (off[low] + high - low) * pad
        return picked[g][at : at + pad, :]

    def products(g, start, stop):
        for i in range(start, stop, 2):
            first = jnp.zeros((2, order, pad, LANES), F32)
            for p in range(order):
                block = jnp.stack([entry(g, min(p, q), max(p, q)) for q in range(order)])
                first = first + c4[g, i : i + 2, p][:, None] * block[None]
            total = first[:, 0][:, None] * c4[g, i:, 0][None]
            for q in range(1, order):
                total = total + first[:, q][:, None] * c4[g, i:, q][None]
            total = total.astype(BF16).astype(F32)
            for n in range(2):
                pscr[g, off[i + n] * pad : (off[i + n] + order - i - n) * pad, :] = total[
                    n, n:
                ].reshape(-1, LANES)

    @pl.when(even & has_above)
    def _():
        pl.semaphore_wait(side_sem, 1)
        halo_copy(0).start()

    @pl.when(near_above > 0)
    def _():
        pl.semaphore_wait(near_sem, near_above)

    for d in range(1, reach + 1):

        @pl.when(me + d < ne)
        def _():
            green_copy(d).start()

    products(0, 0, order)

    load_weight.wait()
    load_shift.wait()

    def add_weights(w, sums):
        shift = shift_ref[w]
        low, high = weight_ref[w], weight_ref[freqs + w]
        new = []
        for d in range(1, reach + 1):
            pick = jnp.where(shift == d, 1.0, 0.0).astype(F32)
            new += [sums[2 * d - 2] + pick * low, sums[2 * d - 1] + pick * high]
        return tuple(new)

    sums = lax.fori_loop(
        0, freqs, add_weights, tuple(jnp.zeros((nbr, atoms), F32) for _ in range(2 * reach)),
        unroll=4,
    )
    for s in range(2 * reach):
        ab[s] = sums[s]

    def rows_of(g, t, j, start, stop):
        at = start * pad + t * len(groups[g]) + j
        return pscr[g, pl.ds(at, stop - start, stride=pad), :]

    def partials(g, t, s, start, stop):
        lanes = slice(t * LANES, (t + 1) * LANES)
        total = None
        for j, k in enumerate(groups[g]):
            term = ab[s, k : k + 1, lanes] * rows_of(g, t, j, start, stop)
            total = term if total is None else total + term
        return total

    for t in range(tiles):
        for s in range(2 * reach):
            pacc[s, :, t * LANES : (t + 1) * LANES] = partials(0, t, s, 0, packed)

    g16[...] = jnp.zeros_like(g16)
    for p in range(order):
        g16[p, :order, :] = green_ref[p].astype(F32)
    sig_ref[...] = jnp.zeros_like(sig_ref)

    @pl.when(has_above)
    def _():
        halo_copy(1).wait_recv()
        pick_neighbours(1, 1, halo[1], hots[1])

    @pl.when(has_below)
    def _():
        halo_copy(0).wait_recv()
        pick_neighbours(1, 0, halo[0], hots[0])


    send_order = [(1 - 2 * (d % 2 == 0)) * d for d in range(1, reach + 1)]
    send_order += [-d for d in send_order]

    def correlations():
        @pl.when(far_above > 0)
        def _():
            pl.semaphore_wait(far_sem, far_above)

        wait_gin(False)

        index = lax.broadcasted_iota(jnp.int32, (packed, LANES), 0)
        twice = jnp.full((packed, LANES), 2.0, F32)
        for p in range(order):
            twice = jnp.where(index == off[p], 1.0, twice)
        rows = [[None] * tiles for _ in range(reach * nbr)]

        def correlate(g, start, stop):
            for t in range(tiles):
                lanes = slice(t * LANES, (t + 1) * LANES)
                greens = [
                    gin[d, start:stop, lanes].astype(F32) * twice[start:stop] for d in range(reach)
                ]
                for j, k in enumerate(groups[g]):
                    value = rows_of(g, t, j, start, stop)
                    for d in range(reach):
                        term = jnp.sum(greens[d] * value, axis=0, keepdims=True)
                        old = rows[d * nbr + k][t]
                        rows[d * nbr + k][t] = term if old is None else old + term

        correlate(0, 0, packed)
        correlate(1, 0, packed)
        sums = [jnp.concatenate([r[t] for r in rows], axis=0) for t in range(tiles)]
        lane = lax.broadcasted_iota(jnp.int32, sums[0].shape, 1)
        for e in range(ne):
            start = e * share % LANES
            low, high = e * share // LANES, (e * share + share - 1) // LANES
            chunks[e] = sums[low] if low == high else jnp.where(lane >= start, sums[low], sums[high])
        for r in range(1, ne):
            chunk_copy(r).start()

    for n, (start, stop, first, final) in enumerate(plan):
        if first < final:
            products(1, first, final)
            if final == order:
                correlations()
        for t in range(tiles):
            lanes = slice(t * LANES, (t + 1) * LANES)
            for s in range(2 * reach):
                total = pacc[s, start:stop, lanes] + partials(1, t, s, start, stop)
                pout[s, start:stop, lanes] = total.astype(BF16)
        for d in send_order:
            if d > 0:

                @pl.when(me + d < ne)
                def _():
                    part_copy(2 * d - 2, n, me + d).start()
            else:

                @pl.when(me >= -d)
                def _():
                    part_copy(-2 * d - 1, n, me + d).start()

    for n, (start, stop, _, _) in enumerate(plan):
        first, final = complete(order, start), complete(order, stop)
        wait_parts(pl.ds(start, stop - start), n, False)
        sigma = pin[0, start:stop].astype(F32)
        for s in range(1, 2 * reach):
            sigma = sigma + pin[s, start:stop].astype(F32)
        sig_ref[start:stop, :] = sigma.astype(BF16)
        s16[first:final] = jnp.dot(
            e16_ref[first * depth : final * depth, :], sig_ref[...], preferred_element_type=F32
        ).reshape(final - first, depth, atoms)
        for i in range(0, order, 2):
            left = [None if first == 0 else l16[i + m] for m in range(2)]
            for p in range(first, final):
                block = s16[p]
                for m in range(2):
                    term = g16[i + m, p : p + 1, :] * block
                    left[m] = term if left[m] is None else left[m] + term
            for m in range(2):
                l16[i + m] = left[m].astype(BF16).astype(F32) if stop == packed else left[m]

    for i in range(0, order, 2):
        total = [g16[i + n] for n in range(2)]
        for p in range(order):
            block = g16[p]
            total = [total[n] + l16[i + n, p : p + 1, :] * block for n in range(2)]
        for n in range(2):
            cor_ref[i + n] = total[n][:order].astype(BF16)

    wait_chunks().wait_recv()
    summed = chunks[me]
    for r in range(1, ne):
        summed = summed + cin[r]
    summed = pltpu.roll(summed, lax.rem(ne * LANES - me * share, LANES), 1)
    summed = summed[:, :share] * (1.0 / (order * math.sqrt(ne)))
    for w in range(freqs):
        shift = shift_ref[w]
        value = jnp.zeros((nbr, share), F32)
        for d in range(1, reach + 1):
            value = jnp.where(shift == d, summed[(d - 1) * nbr : d * nbr], value)
        pol_ref[w] = value

    for c in range(1, 3):

        @pl.when(has_above.astype(jnp.int32) + has_below.astype(jnp.int32) == c)
        def _():
            some = halo.at[pl.ds(0, c)]
            remote(some, some, halo_send.at[0], halo_recv.at[0], me, layer).wait_send()

    wait_gin(True)
    wait_parts(pl.ds(0, packed), 0, True)
    wait_chunks().wait_send()


def finish(cor_ref, pol_ref, cor_hbm, pol_hbm, sem):
    first = pltpu.make_async_copy(cor_ref, cor_hbm, sem.at[0])
    second = pltpu.make_async_copy(pol_ref, pol_hbm, sem.at[1])
    first.start()
    second.start()
    first.wait()
    second.wait()


def body(green_blocks, coupling, phonon_weights, neighbours, phonon_shifts):
    ne = lax.axis_size("energy")
    reach = max(ne // 4, 1)
    order = green_blocks.shape[1]
    atoms = green_blocks.shape[3]
    nbr = neighbours.shape[0]
    freqs = phonon_shifts.shape[0]
    tiles = atoms // LANES
    share = atoms // ne
    count = order * (order + 1) // 2
    packed = -(-count // 16) * 16
    pad = -(-(tiles * max(nbr - 2, 2)) // 8) * 8
    rows = 16 * (-(-order // 16))
    parts = len(segments(order, packed))
    vmem = pl.BlockSpec(memory_space=pltpu.VMEM)
    hbm = pl.BlockSpec(memory_space=pltpu.HBM)
    dma = pltpu.SemaphoreType.DMA
    green = green_blocks[0]
    staged = pl.pallas_call(
        functools.partial(kernel, reach),
        out_shape=(
            jax.ShapeDtypeStruct((order, order, atoms), BF16),
            jax.ShapeDtypeStruct((freqs, nbr, share), F32),
        ),
        in_specs=[hbm] * 5,
        out_specs=(vmem, vmem),
        scratch_shapes=[
            pltpu.SMEM((freqs,), jnp.int32),
            pltpu.VMEM((order, order, atoms), BF16),
            pltpu.VMEM((order * order, nbr, atoms), BF16),
            pltpu.VMEM((2 * freqs, nbr, atoms), F32),
            pltpu.VMEM((nbr, atoms), jnp.int32),
            pltpu.VMEM((order * rows, packed), BF16),
            pltpu.VMEM((packed, atoms), BF16),
            pltpu.VMEM((order, rows, atoms), F32),
            pltpu.VMEM((order, rows, atoms), F32),
            pltpu.VMEM((order, rows, atoms), F32),
            pltpu.VMEM((packed, atoms), F32),
            pltpu.VMEM((packed, atoms), BF16),
            pltpu.VMEM((2, packed, atoms), BF16),
            pltpu.VMEM((reach, packed, atoms), BF16),
            pltpu.VMEM((2 * reach, packed, atoms), BF16),
            pltpu.VMEM((2 * reach, packed, atoms), BF16),
            pltpu.VMEM((2 * reach, packed, atoms), F32),
            pltpu.VMEM((2, atoms, atoms), BF16),
            pltpu.VMEM((ne, reach * nbr, LANES), F32),
            pltpu.VMEM((ne, reach * nbr, LANES), F32),
            pltpu.VMEM((2, order, order, pad, LANES), F32),
            pltpu.VMEM((packed * pad, LANES), F32),
            pltpu.VMEM((packed * pad, LANES), F32),
            pltpu.VMEM((2, packed * pad, LANES), F32),
            pltpu.VMEM((2 * reach, nbr, atoms), F32),
            dma((5,)), *[pltpu.SemaphoreType.REGULAR] * 3,
            dma((1,)), dma((2,)), dma((1,)), dma((1,)), dma((1,)), dma((parts,)), dma((1,)), dma((1,)),
        ],
        compiler_params=pltpu.CompilerParams(
            collective_id=0, has_side_effects=True, vmem_limit_bytes=VMEM_LIMIT
        ),
    )(
        *(
            pltpu.with_memory_space_constraint(x, pltpu.HBM)
            for x in (
                phonon_shifts,
                green,
                coupling.reshape(order * order, nbr, atoms),
                phonon_weights.reshape(2 * freqs, nbr, atoms),
                neighbours,
            )
        )
    )
    corrected, polarization = pl.pallas_call(
        finish,
        out_shape=(
            jax.ShapeDtypeStruct((order, order, atoms), BF16),
            jax.ShapeDtypeStruct((freqs, nbr, share), F32),
        ),
        in_specs=[vmem, vmem],
        out_specs=(hbm, hbm),
        scratch_shapes=[dma((2,))],
        compiler_params=pltpu.CompilerParams(vmem_limit_bytes=VMEM_LIMIT),
    )(*staged)
    return corrected[None], polarization


def solution(mesh):
    return jax.shard_map(
        body,
        mesh=mesh,
        in_specs=(
            P("energy", None, None, "layer"),
            P(None, None, None, "layer"),
            P(None, None, None, "layer"),
            P(None, "layer"),
            P(),
        ),
        out_specs=(P("energy", None, None, "layer"), P(None, None, ("layer", "energy"))),
        check_vma=False,
    )
```

```python
import functools
import math

import jax
import jax.numpy as jnp
from jax import lax
from jax.experimental import pallas as pl
from jax.experimental.pallas import tpu as pltpu
from jax.sharding import PartitionSpec as P

MESH = pl.DeviceIdType.MESH
LANES = 128
F32 = jnp.float32
BF16 = jnp.bfloat16
VMEM_LIMIT = 48 * 1024 * 1024


def offsets(order):
    return [p * order - p * (p - 1) // 2 for p in range(order)]


def segments(order, packed):
    stops = [16] + [o // 16 * 16 for o in offsets(order)[4::4]] + [packed]
    plan, start, first = [], 0, 0
    for stop in stops:
        if stop > start:
            final = 2 if start == 0 else order
            plan.append((start, stop, first, final))
            start, first = stop, final
    return plan


def complete(order, stop):
    return sum(o + order - p <= stop for p, o in enumerate(offsets(order)))


def expansion(order, row_stride, packed_rows):
    row = lax.broadcasted_iota(jnp.int32, (order * row_stride, packed_rows), 0)
    column = lax.broadcasted_iota(jnp.int32, (order * row_stride, packed_rows), 1)
    p, q = row // row_stride, row % row_stride
    low, high = jnp.minimum(p, q), jnp.maximum(p, q)
    entry = low * order - low * (low - 1) // 2 + high - low
    return jnp.where((entry == column) & (q < order), 1.0, 0.0).astype(BF16)


def kernel(
    reach, shift_hbm, green_hbm, coup_hbm, weight_hbm, near_hbm, cor_ref, pol_ref,
    shift_ref, green_ref, coup_ref, weight_ref, near_ref, e16_ref, sig_ref,
    g16, s16, l16, tri32, own, halo, gin, pout, pin, pacc, hots, chunks, cin, c4, g3, pscr, cx, cp, gs, ps, ab, aw,
    load_sem, side_sem, near_sem, far_sem, halo_send, halo_recv, gin_send, gin_recv, part_send, part_recv,
    chunk_send, chunk_recv,
):
    order = green_ref.shape[0]
    atoms = green_ref.shape[2]
    nbr = near_ref.shape[0]
    freqs = shift_ref.shape[0]
    tiles = atoms // LANES
    packed = own.shape[0]
    pad = c4.shape[2]
    fold = cx.shape[3]
    ne = lax.axis_size("energy")
    nl = lax.axis_size("layer")
    me = lax.axis_index("energy")
    layer = lax.axis_index("layer")
    share = atoms // ne
    depth = s16.shape[1]
    off = offsets(order)
    plan = segments(order, packed)
    slots = tuple(range(2, nbr))
    size = len(slots)

    def load(n, src, dst):
        copy = pltpu.make_async_copy(src, dst, load_sem.at[n])
        copy.start()
        return copy

    step = order // 4
    for p in range(0, order, step):
        load(0, green_hbm.at[pl.ds(p, step)], green_ref.at[pl.ds(p, step)])
    load_green = pltpu.make_async_copy(green_hbm, green_ref, load_sem.at[0])
    load_near = load(1, near_hbm, near_ref)
    load_coup = load(2, coup_hbm, coup_ref)
    load_weight = load(3, weight_hbm, weight_ref)
    load_shift = load(4, shift_hbm, shift_ref)

    barrier = pltpu.get_barrier_semaphore()

    def greet(sem, energy, row):
        pl.semaphore_signal(
            sem, inc=1, device_id={"energy": energy, "layer": row}, device_id_type=MESH
        )

    odd = lax.rem(me, 2) == 1
    even = jnp.logical_not(odd)
    has_above, has_below = layer < nl - 1, layer > 0
    near_above = jnp.minimum(ne - 1 - me, reach)
    near_count = near_above + jnp.minimum(me, reach)
    far_above = ne - 1 - me - near_above

    for d in range(1, ne):

        @pl.when(me + d < ne)
        def _():
            greet(barrier, me + d, layer)

    @pl.when(has_above)
    def _():
        greet(barrier, me, layer + 1)

    @pl.when(has_below)
    def _():
        greet(barrier, me - lax.rem(me, 2) + 1, layer - 1)

    @pl.when(odd)
    def _():
        greet(barrier, me - 1, layer)

    tri32[...] = jnp.zeros_like(tri32)
    load_green.wait()
    for p in range(order):
        tri32[off[p] : off[p] + order - p, :] = green_ref[p].astype(F32)[p:, :]
    own[...] = tri32[...].astype(BF16)

    pl.semaphore_wait(
        barrier,
        me
        + even.astype(jnp.int32)
        + has_below.astype(jnp.int32)
        + 2 * (odd & has_above).astype(jnp.int32),
    )

    def remote(src, dst, send, recv, energy, row):
        return pltpu.make_async_remote_copy(
            src_ref=src, dst_ref=dst, send_sem=send, recv_sem=recv,
            device_id={"energy": energy, "layer": row}, device_id_type=MESH,
        )

    def halo_copy(side):
        row = layer + 1 if side == 0 else layer - 1
        return remote(own, halo.at[side], halo_send.at[0], halo_recv.at[side], me, row)

    def green_copy(d):
        return remote(
            own, gin.at[d - 1], gin_send.at[0], gin_recv.at[0], me + d, layer
        )

    def part_copy(slot, n, energy):
        start, stop, _, _ = plan[n]
        rows = pl.ds(start, stop - start)
        return remote(
            pout.at[slot, rows], pin.at[slot, rows], part_send.at[0], part_recv.at[n],
            energy, layer,
        )

    def chunk_copy(r):
        dest = lax.rem(me + r, ne)
        return remote(
            chunks.at[dest], cin.at[r], chunk_send.at[0], chunk_recv.at[0], dest, layer
        )

    def wait_gin(send):
        number = jnp.minimum(ne - 1 - me, reach) if send else jnp.minimum(me, reach)
        for c in range(1, reach + 1):

            @pl.when(number == c)
            def _():
                some = gin.at[pl.ds(0, c)]
                copy = remote(some, some, gin_send.at[0], gin_recv.at[0], me, layer)
                copy.wait_send() if send else copy.wait_recv()

    def wait_parts(rows, recv, send):
        for c in range(1, 2 * reach + 1):

            @pl.when(near_count == c)
            def _():
                some = pin.at[pl.ds(0, c), rows]
                copy = remote(some, some, part_send.at[0], part_recv.at[recv], me, layer)
                copy.wait_send() if send else copy.wait_recv()

    def wait_chunks():
        some = cin.at[pl.ds(1, ne - 1)]
        return remote(some, some, chunk_send.at[0], chunk_recv.at[0], me, layer)

    @pl.when(has_below)
    def _():
        halo_copy(1).start()

    @pl.when(odd & has_above)
    def _():
        halo_copy(0).start()
        greet(side_sem, me - 1, layer)

    for d in range(1, ne):

        @pl.when(me >= d)
        def _():
            greet(near_sem if d <= reach else far_sem, me - d, layer)

    row = lax.broadcasted_iota(jnp.int32, (atoms, atoms), 0)

    def one_hot(k, start):
        return jnp.where(row == near_ref[k : k + 1, :] - start, 1.0, 0.0).astype(BF16)

    def taken(blocks, hot):
        found = jnp.dot(blocks, hot, preferred_element_type=F32)
        return [found[:, t * LANES : (t + 1) * LANES] for t in range(tiles)]

    def pick_side(side):
        for t, found in enumerate(taken(halo[side], hots[side])):
            for n in range(2):
                gs[side, pl.ds(n * tiles + t, packed, stride=fold), :] = found

    load_near.wait()
    for j, k in enumerate(slots):
        for t, found in enumerate(taken(own[...], one_hot(k, atoms))):
            g3[pl.ds(t * size + j, packed, stride=pad), :] = found
    hots[0] = one_hot(0, 0)
    hots[1] = one_hot(1, 2 * atoms)

    @pl.when(even & has_above)
    def _():
        pl.semaphore_wait(side_sem, 1)
        halo_copy(0).start()

    @pl.when(near_above > 0)
    def _():
        pl.semaphore_wait(near_sem, near_above)

    for d in range(1, reach + 1):

        @pl.when(me + d < ne)
        def _():
            green_copy(d).start()

    both = has_above & has_below
    lower_first = lax.rem(layer, 2) == 1
    early = jnp.where(both, jnp.where(lower_first, 0, 1), jnp.where(has_above, 0, 1))
    late = 1 - early

    @pl.when(jnp.logical_not(both))
    def _():
        ps[early] = jnp.zeros(ps.shape[1:], F32)

    for d in range(1, reach + 1):

        @pl.when(me < d)
        def _():
            gin[d - 1] = jnp.zeros((packed, atoms), BF16)
            pin[2 * d - 2] = jnp.zeros(pin.shape[1:], BF16)

        @pl.when(me + d >= ne)
        def _():
            pin[2 * d - 1] = jnp.zeros(pin.shape[1:], BF16)

    e16_ref[...] = expansion(order, depth, packed)
    load_coup.wait()
    for t in range(tiles):
        block = coup_ref[:, :, t * LANES : (t + 1) * LANES].astype(F32)
        block = block.reshape(order, order, nbr, LANES)
        c4[:, :, t * size : (t + 1) * size, :] = block[:, :, slots[0] :, :]
        for side in range(2):
            for n in range(2):
                at = n * tiles + t
                cx[side, :, :, at : at + 1, :] = block[:, :, side : side + 1, :]
    lower = lax.broadcasted_iota(jnp.int32, (order, fold, LANES), 1) < tiles
    for side in range(2):
        for i in range(0, order, 2):
            cp[side, i // 2] = jnp.where(lower, cx[side, i], cx[side, i + 1])

    last = off[-1] + 1
    pscr[last * pad :, :] = jnp.zeros(((packed - last) * pad, LANES), F32)
    for side in range(2):
        ps[side, last * fold :, :] = jnp.zeros(((packed - last) * fold, LANES), F32)

    def entries(p, rows):
        at = [off[min(p, q)] + abs(p - q) for q in range(order)]
        return [slice(a * rows, (a + 1) * rows) for a in at]

    def products():
        for i in range(0, order, 2):
            first = jnp.zeros((2, order, pad, LANES), F32)
            for p in range(order):
                block = jnp.stack([g3[at, :] for at in entries(p, pad)])
                first = first + c4[i : i + 2, p][:, None] * block[None]
            total = first[:, 0][:, None] * c4[i:, 0][None]
            for q in range(1, order):
                total = total + first[:, q][:, None] * c4[i:, q][None]
            total = total.astype(BF16).astype(F32)
            for n in range(2):
                pscr[off[i + n] * pad : (off[i + n] + order - i - n) * pad, :] = total[
                    n, n:
                ].reshape(-1, LANES)

    def side_products(side, start, stop):
        for i in range(start, stop, 2):
            first = jnp.zeros((order, fold, LANES), F32)
            for p in range(order):
                block = jnp.stack([gs[side, at, :] for at in entries(p, fold)])
                first = first + cp[side, i // 2, p][None] * block
            total = first[0][None] * cx[side, i:, 0]
            for q in range(1, order):
                total = total + first[q][None] * cx[side, i:, q]
            total = total.astype(BF16).astype(F32).reshape(-1, LANES)
            ps[side, off[i] * fold : off[i + 1] * fold, :] = total
            second = total[fold:].reshape(-1, fold, LANES)
            second = jnp.concatenate([second[:, tiles:], second[:, :tiles]], axis=1)
            ps[side, off[i + 1] * fold : (off[i + 1] + order - i - 1) * fold, :] = second.reshape(
                -1, LANES
            )

    products()

    load_weight.wait()
    load_shift.wait()

    def add_weights(w, sums):
        shift = shift_ref[w]
        low, high = weight_ref[w], weight_ref[freqs + w]
        new = []
        for d in range(1, reach + 1):
            pick = jnp.where(shift == d, 1.0, 0.0).astype(F32)
            new += [sums[2 * d - 2] + pick * low, sums[2 * d - 1] + pick * high]
        return tuple(new)

    sums = lax.fori_loop(
        0, freqs, add_weights, tuple(jnp.zeros((nbr, atoms), F32) for _ in range(2 * reach)),
        unroll=4,
    )
    for s in range(2 * reach):
        ab[s] = sums[s]
        for side in range(2):
            aw[side, s] = jnp.broadcast_to(sums[s][side : side + 1], aw.shape[2:])

    def rows_of(j, t, start, stop):
        at = start * pad + t * size + j
        return pscr[pl.ds(at, stop - start, stride=pad), :]

    def side_rows(side, t, start, stop):
        return ps[side, pl.ds(start * fold + t, stop - start, stride=fold), :]

    def side_partials(side, t, s, start, stop):
        lanes = slice(t * LANES, (t + 1) * LANES)
        weight = aw[side, s, 0:1, lanes]
        return pacc[s, start:stop, lanes] + weight * side_rows(side, t, start, stop)

    for t in range(tiles):
        lanes = slice(t * LANES, (t + 1) * LANES)
        for s in range(2 * reach):
            total = None
            for j, k in enumerate(slots):
                term = ab[s, k : k + 1, lanes] * rows_of(j, t, 0, packed)
                total = term if total is None else total + term
            pacc[s, :, lanes] = total

    g16[...] = jnp.zeros_like(g16)
    for p in range(order):
        g16[p, :order, :] = green_ref[p].astype(F32)
    sig_ref[...] = jnp.zeros_like(sig_ref)

    @pl.when(both & lower_first)
    def _():
        halo_copy(0).wait_recv()

    @pl.when(both & jnp.logical_not(lower_first))
    def _():
        halo_copy(1).wait_recv()

    @pl.when(both)
    def _():
        pick_side(early)
        side_products(early, 0, order)
        for t in range(tiles):
            for s in range(2 * reach):
                pacc[s, :, t * LANES : (t + 1) * LANES] = side_partials(early, t, s, 0, packed)

    @pl.when(late == 0)
    def _():
        halo_copy(0).wait_recv()

    @pl.when(late == 1)
    def _():
        halo_copy(1).wait_recv()

    pick_side(late)

    send_order = [(1 - 2 * (d % 2 == 0)) * d for d in range(1, reach + 1)]
    send_order += [-d for d in send_order]

    def correlations():
        @pl.when(far_above > 0)
        def _():
            pl.semaphore_wait(far_sem, far_above)

        wait_gin(False)

        index = lax.broadcasted_iota(jnp.int32, (packed, LANES), 0)
        twice = jnp.full((packed, LANES), 2.0, F32)
        for p in range(order):
            twice = jnp.where(index == off[p], 1.0, twice)
        rows = [[None] * tiles for _ in range(reach * nbr)]

        for t in range(tiles):
            greens = [
                gin[d, :, t * LANES : (t + 1) * LANES].astype(F32) * twice for d in range(reach)
            ]
            for k in range(nbr):
                if k < 2:
                    value = side_rows(k, t, 0, packed)
                else:
                    value = rows_of(k - 2, t, 0, packed)
                for d in range(reach):
                    rows[d * nbr + k][t] = jnp.sum(greens[d] * value, axis=0, keepdims=True)

        sums = [jnp.concatenate([r[t] for r in rows], axis=0) for t in range(tiles)]
        lane = lax.broadcasted_iota(jnp.int32, sums[0].shape, 1)
        for e in range(ne):
            start = e * share % LANES
            low, high = e * share // LANES, (e * share + share - 1) // LANES
            chunks[e] = sums[low] if low == high else jnp.where(lane >= start, sums[low], sums[high])
        for r in range(1, ne):
            chunk_copy(r).start()

    for n, (start, stop, first, final) in enumerate(plan):
        if first < final:
            side_products(late, first, final)
            if final == order:
                correlations()
        for t in range(tiles):
            lanes = slice(t * LANES, (t + 1) * LANES)
            for s in range(2 * reach):
                pout[s, start:stop, lanes] = side_partials(late, t, s, start, stop).astype(BF16)
        for d in send_order:
            if d > 0:

                @pl.when(me + d < ne)
                def _():
                    part_copy(2 * d - 2, n, me + d).start()
            else:

                @pl.when(me >= -d)
                def _():
                    part_copy(-2 * d - 1, n, me + d).start()

    for n, (start, stop, _, _) in enumerate(plan):
        first, final = complete(order, start), complete(order, stop)
        wait_parts(pl.ds(start, stop - start), n, False)
        sigma = pin[0, start:stop].astype(F32)
        for s in range(1, 2 * reach):
            sigma = sigma + pin[s, start:stop].astype(F32)
        sig_ref[start:stop, :] = sigma.astype(BF16)
        s16[first:final] = jnp.dot(
            e16_ref[first * depth : final * depth, :], sig_ref[...], preferred_element_type=F32
        ).reshape(final - first, depth, atoms)
        for i in range(0, order, 2):
            left = [None if first == 0 else l16[i + m] for m in range(2)]
            for p in range(first, final):
                block = s16[p]
                for m in range(2):
                    term = g16[i + m, p : p + 1, :] * block
                    left[m] = term if left[m] is None else left[m] + term
            for m in range(2):
                l16[i + m] = left[m].astype(BF16).astype(F32) if stop == packed else left[m]

    for i in range(0, order, 2):
        total = [g16[i + n] for n in range(2)]
        for p in range(order):
            block = g16[p]
            total = [total[n] + l16[i + n, p : p + 1, :] * block for n in range(2)]
        for n in range(2):
            cor_ref[i + n] = total[n][:order].astype(BF16)

    wait_chunks().wait_recv()
    summed = chunks[me]
    for r in range(1, ne):
        summed = summed + cin[r]
    summed = pltpu.roll(summed, lax.rem(ne * LANES - me * share, LANES), 1)
    summed = summed[:, :share] * (1.0 / (order * math.sqrt(ne)))
    for w in range(freqs):
        shift = shift_ref[w]
        value = jnp.zeros((nbr, share), F32)
        for d in range(1, reach + 1):
            value = jnp.where(shift == d, summed[(d - 1) * nbr : d * nbr], value)
        pol_ref[w] = value

    for c in range(1, 3):

        @pl.when(has_above.astype(jnp.int32) + has_below.astype(jnp.int32) == c)
        def _():
            some = halo.at[pl.ds(0, c)]
            remote(some, some, halo_send.at[0], halo_recv.at[0], me, layer).wait_send()

    wait_gin(True)
    wait_parts(pl.ds(0, packed), 0, True)
    wait_chunks().wait_send()


def finish(cor_ref, pol_ref, cor_hbm, pol_hbm, sem):
    first = pltpu.make_async_copy(cor_ref, cor_hbm, sem.at[0])
    second = pltpu.make_async_copy(pol_ref, pol_hbm, sem.at[1])
    first.start()
    second.start()
    first.wait()
    second.wait()


def body(green_blocks, coupling, phonon_weights, neighbours, phonon_shifts):
    ne = lax.axis_size("energy")
    reach = max(ne // 4, 1)
    order = green_blocks.shape[1]
    atoms = green_blocks.shape[3]
    nbr = neighbours.shape[0]
    freqs = phonon_shifts.shape[0]
    tiles = atoms // LANES
    share = atoms // ne
    count = order * (order + 1) // 2
    packed = -(-count // 16) * 16
    pad = -(-(tiles * (nbr - 2)) // 8) * 8
    fold = -(-(2 * tiles) // 8) * 8
    rows = 16 * (-(-order // 16))
    parts = len(segments(order, packed))
    vmem = pl.BlockSpec(memory_space=pltpu.VMEM)
    hbm = pl.BlockSpec(memory_space=pltpu.HBM)
    dma = pltpu.SemaphoreType.DMA
    green = green_blocks[0]
    staged = pl.pallas_call(
        functools.partial(kernel, reach),
        out_shape=(
            jax.ShapeDtypeStruct((order, order, atoms), BF16),
            jax.ShapeDtypeStruct((freqs, nbr, share), F32),
        ),
        in_specs=[hbm] * 5,
        out_specs=(vmem, vmem),
        scratch_shapes=[
            pltpu.SMEM((freqs,), jnp.int32),
            pltpu.VMEM((order, order, atoms), BF16),
            pltpu.VMEM((order * order, nbr, atoms), BF16),
            pltpu.VMEM((2 * freqs, nbr, atoms), F32),
            pltpu.VMEM((nbr, atoms), jnp.int32),
            pltpu.VMEM((order * rows, packed), BF16),
            pltpu.VMEM((packed, atoms), BF16),
            pltpu.VMEM((order, rows, atoms), F32),
            pltpu.VMEM((order, rows, atoms), F32),
            pltpu.VMEM((order, rows, atoms), F32),
            pltpu.VMEM((packed, atoms), F32),
            pltpu.VMEM((packed, atoms), BF16),
            pltpu.VMEM((2, packed, atoms), BF16),
            pltpu.VMEM((reach, packed, atoms), BF16),
            pltpu.VMEM((2 * reach, packed, atoms), BF16),
            pltpu.VMEM((2 * reach, packed, atoms), BF16),
            pltpu.VMEM((2 * reach, packed, atoms), F32),
            pltpu.VMEM((2, atoms, atoms), BF16),
            pltpu.VMEM((ne, reach * nbr, LANES), F32),
            pltpu.VMEM((ne, reach * nbr, LANES), F32),
            pltpu.VMEM((order, order, pad, LANES), F32),
            pltpu.VMEM((packed * pad, LANES), F32),
            pltpu.VMEM((packed * pad, LANES), F32),
            pltpu.VMEM((2, order, order, fold, LANES), F32),
            pltpu.VMEM((2, order // 2, order, fold, LANES), F32),
            pltpu.VMEM((2, packed * fold, LANES), F32),
            pltpu.VMEM((2, packed * fold, LANES), F32),
            pltpu.VMEM((2 * reach, nbr, atoms), F32),
            pltpu.VMEM((2, 2 * reach, 8, atoms), F32),
            dma((5,)), *[pltpu.SemaphoreType.REGULAR] * 3,
            dma((1,)), dma((2,)), dma((1,)), dma((1,)), dma((1,)), dma((parts,)), dma((1,)), dma((1,)),
        ],
        compiler_params=pltpu.CompilerParams(
            collective_id=0, has_side_effects=True, vmem_limit_bytes=VMEM_LIMIT
        ),
    )(
        *(
            pltpu.with_memory_space_constraint(x, pltpu.HBM)
            for x in (
                phonon_shifts,
                green,
                coupling.reshape(order * order, nbr, atoms),
                phonon_weights.reshape(2 * freqs, nbr, atoms),
                neighbours,
            )
        )
    )
    corrected, polarization = pl.pallas_call(
        finish,
        out_shape=(
            jax.ShapeDtypeStruct((order, order, atoms), BF16),
            jax.ShapeDtypeStruct((freqs, nbr, share), F32),
        ),
        in_specs=[vmem, vmem],
        out_specs=(hbm, hbm),
        scratch_shapes=[dma((2,))],
        compiler_params=pltpu.CompilerParams(vmem_limit_bytes=VMEM_LIMIT),
    )(*staged)
    return corrected[None], polarization


def solution(mesh):
    return jax.shard_map(
        body,
        mesh=mesh,
        in_specs=(
            P("energy", None, None, "layer"),
            P(None, None, None, "layer"),
            P(None, None, None, "layer"),
            P(None, "layer"),
            P(),
        ),
        out_specs=(P("energy", None, None, "layer"), P(None, None, ("layer", "energy"))),
        check_vma=False,
    )
```

```python
import functools
import math

import jax
import jax.numpy as jnp
from jax import lax
from jax.experimental import pallas as pl
from jax.experimental.pallas import tpu as pltpu
from jax.sharding import PartitionSpec as P

MESH = pl.DeviceIdType.MESH
LANES = 128
F32 = jnp.float32
BF16 = jnp.bfloat16
VMEM_LIMIT = 48 * 1024 * 1024


def offsets(order):
    return [p * order - p * (p - 1) // 2 for p in range(order)]


def segments(order, packed):
    stops = [16] + [o // 16 * 16 for o in offsets(order)[4::4]] + [packed]
    plan, start, first = [], 0, 0
    for stop in stops:
        if stop > start:
            final = 2 if start == 0 else order
            plan.append((start, stop, first, final))
            start, first = stop, final
    return plan


def routes(reach):
    straight, shared = ([], []), []
    for d in range(1, (reach + 1) // 2 + 1):
        for way in (1, -1):
            slot = 2 * d - (way > 0)
            for parity in range(2):
                far = [abs(2 * d * way + parity - p) for p in range(2)]
                near = [p for p in range(2) if far[p] <= reach]
                if len(near) == 2:
                    shared.append((2 * d * way + parity, slot))
                elif near:
                    straight[near[0]].append((2 * d * way + parity - near[0], slot))
    return straight, shared


def complete(order, stop):
    return sum(o + order - p <= stop for p, o in enumerate(offsets(order)))


def expansion(order, row_stride, packed_rows):
    row = lax.broadcasted_iota(jnp.int32, (order * row_stride, packed_rows), 0)
    column = lax.broadcasted_iota(jnp.int32, (order * row_stride, packed_rows), 1)
    p, q = row // row_stride, row % row_stride
    low, high = jnp.minimum(p, q), jnp.maximum(p, q)
    entry = low * order - low * (low - 1) // 2 + high - low
    return jnp.where((entry == column) & (q < order), 1.0, 0.0).astype(BF16)


def kernel(
    reach, shift_hbm, green_hbm, coup_hbm, weight_hbm, near_hbm, cor_ref, pol_ref,
    shift_ref, green_ref, coup_ref, weight_ref, near_ref, e16_ref, sig_ref,
    g16, s16, l16, tri32, own, halo, gin, pout, pin, given, landing, pacc, hots, chunks, cin, c4, g3, pscr, cx, cp, gs, ps, ab, aw,
    load_sem, side_sem, near_sem, far_sem, sent_sem, halo_recv, gin_recv, part_recv, share_recv,
    chunk_send, chunk_recv,
):
    order = green_ref.shape[0]
    atoms = green_ref.shape[2]
    nbr = near_ref.shape[0]
    freqs = shift_ref.shape[0]
    tiles = atoms // LANES
    packed = own.shape[0]
    pad = c4.shape[2]
    fold = cx.shape[3]
    ne = lax.axis_size("energy")
    nl = lax.axis_size("layer")
    me = lax.axis_index("energy")
    layer = lax.axis_index("layer")
    share = atoms // ne
    depth = s16.shape[1]
    off = offsets(order)
    plan = segments(order, packed)
    slots = tuple(range(2, nbr))
    size = len(slots)

    def load(n, src, dst):
        copy = pltpu.make_async_copy(src, dst, load_sem.at[n])
        copy.start()
        return copy

    step = order // 4
    for p in range(0, order, step):
        load(0, green_hbm.at[pl.ds(p, step)], green_ref.at[pl.ds(p, step)])
    load_green = pltpu.make_async_copy(green_hbm, green_ref, load_sem.at[0])
    load_near = load(1, near_hbm, near_ref)
    load_shift = load(2, shift_hbm, shift_ref)

    barrier = pltpu.get_barrier_semaphore()

    def greet(sem, energy, row):
        pl.semaphore_signal(
            sem, inc=1, device_id={"energy": energy, "layer": row}, device_id_type=MESH
        )

    odd = lax.rem(me, 2) == 1
    even = jnp.logical_not(odd)
    relayed = me >= ne - 2
    told = even & relayed
    has_above, has_below = layer < nl - 1, layer > 0
    near_above = jnp.minimum(ne - 1 - me, reach)
    near_count = near_above + jnp.minimum(me, reach)
    far_above = ne - 1 - me - near_above

    @pl.when(has_below)
    def _():
        greet(barrier, me + told.astype(jnp.int32), layer - 1)

    @pl.when(odd)
    def _():
        greet(barrier, me - 1, layer)

    @pl.when(has_above)
    def _():
        greet(barrier, me, layer + 1)

    for d in range(1, ne):

        @pl.when(me + d < ne)
        def _():
            greet(barrier, me + d, layer)

    tri32[...] = jnp.zeros_like(tri32)
    load_green.wait()
    load_coup = load(0, coup_hbm, coup_ref)
    for p in range(order):
        tri32[off[p] : off[p] + order - p, :] = green_ref[p].astype(F32)[p:, :]
    own[...] = tri32[...].astype(BF16)

    pl.semaphore_wait(
        barrier,
        me
        + even.astype(jnp.int32)
        + has_below.astype(jnp.int32)
        + jnp.where(told, 0, jnp.where(relayed, 2, 1)) * has_above.astype(jnp.int32),
    )

    def remote(src, dst, send, recv, energy, row):
        return pltpu.make_async_remote_copy(
            src_ref=src, dst_ref=dst, send_sem=send, recv_sem=recv,
            device_id={"energy": energy, "layer": row}, device_id_type=MESH,
        )

    straight, shared = routes(reach)
    base = me - lax.rem(me, 2)

    def reaches(offset):
        return (offset >= 0) & (offset < ne)

    def heard(slot):
        d = (slot + 1) // 2
        if slot % 2:
            return (base >= 2 * d) & (2 * d - even.astype(jnp.int32) <= reach)
        return (base + 2 * d < ne) & (2 * d - odd.astype(jnp.int32) <= reach)

    def number(conditions):
        total = 0
        for condition in conditions:
            total = total + condition.astype(jnp.int32)
        return total

    heard_count = 1 + number([heard(slot) for slot in range(1, pin.shape[0])])
    shared_count = number([reaches(base + e) for e, _ in shared])
    sent_count = 1 + shared_count + near_above + number([has_above, has_below])
    for parity in range(2):
        which = odd if parity else even
        sent_count = sent_count + number([which & reaches(me + e) for e, _ in straight[parity]])

    def halo_copy(side):
        row = layer + 1 if side == 0 else layer - 1
        return remote(own, halo.at[side], sent_sem.at[0], halo_recv.at[side], me, row)

    def green_copy(d):
        return remote(
            own, gin.at[d - 1], sent_sem.at[0], gin_recv.at[0], me + d, layer
        )

    def part_copy(source, target, n, e):
        start, stop, _, _ = plan[n]
        rows = pl.ds(start, stop - start)
        return remote(
            pout.at[source, rows], target.at[rows], sent_sem.at[0],
            part_recv.at[n], me + e, layer,
        )

    def share_copy(source, number, n):
        start, stop, _, _ = plan[n]
        rows = pl.ds(start, stop - start)
        return remote(
            pout.at[source, rows], given.at[number, rows], sent_sem.at[0], share_recv.at[n],
            me + 1, layer,
        )

    def outgoing(offset):
        return 2 * offset - 2 if offset > 0 else -2 * offset - 1

    def chunk_copy(r):
        dest = lax.rem(me + r, ne)
        return remote(
            chunks.at[dest], cin.at[r], chunk_send.at[0], chunk_recv.at[0], dest, layer
        )

    def wait_gin():
        for c in range(1, reach + 1):

            @pl.when(jnp.minimum(me, reach) == c)
            def _():
                some = gin.at[pl.ds(0, c)]
                remote(some, some, sent_sem.at[0], gin_recv.at[0], me, layer).wait_recv()

    def wait_parts(count, most, rows, copy_of):
        for c in range(1, most + 1):

            @pl.when(count == c)
            def _():
                copy_of(landing.at[pl.ds(0, c), rows])

    def wait_heard(rows, n):
        wait_parts(
            heard_count, pin.shape[0], rows,
            lambda some: remote(
                some, some, sent_sem.at[0], part_recv.at[n], me, layer
            ).wait_recv(),
        )

    def wait_shared(rows, n):
        wait_parts(
            shared_count, len(shared), rows,
            lambda some: remote(
                some, some, sent_sem.at[0], share_recv.at[n], me, layer
            ).wait_recv(),
        )

    def wait_sent():
        wait_parts(
            sent_count, landing.shape[0], pl.ds(0, packed),
            lambda some: remote(
                some, some, sent_sem.at[0], part_recv.at[0], me, layer
            ).wait_send(),
        )

    def wait_chunks():
        some = cin.at[pl.ds(1, ne - 1)]
        return remote(some, some, chunk_send.at[0], chunk_recv.at[0], me, layer)

    @pl.when(has_below)
    def _():
        halo_copy(1).start()

    @pl.when(has_above & jnp.logical_not(told))
    def _():
        halo_copy(0).start()

    @pl.when(has_above & odd & relayed)
    def _():
        greet(side_sem, me - 1, layer)

    for d in range(1, ne):

        @pl.when(me >= d)
        def _():
            greet(near_sem if d <= reach else far_sem, me - d, layer)

    row = lax.broadcasted_iota(jnp.int32, (atoms, atoms), 0)

    def one_hot(k, start):
        return jnp.where(row == near_ref[k : k + 1, :] - start, 1.0, 0.0).astype(BF16)

    def taken(blocks, hot):
        found = jnp.dot(blocks, hot, preferred_element_type=F32)
        return [found[:, t * LANES : (t + 1) * LANES] for t in range(tiles)]

    def pick_side(side):
        for t, found in enumerate(taken(halo[side], hots[side])):
            for n in range(2):
                gs[side, pl.ds(n * tiles + t, packed, stride=fold), :] = found

    load_near.wait()
    load_weight = load(1, weight_hbm, weight_ref)
    for j, k in enumerate(slots):
        for t, found in enumerate(taken(own[...], one_hot(k, atoms))):
            g3[pl.ds(t * size + j, packed, stride=pad), :] = found
    hots[0] = one_hot(0, 0)
    hots[1] = one_hot(1, 2 * atoms)

    @pl.when(told & has_above)
    def _():
        pl.semaphore_wait(side_sem, 1)
        halo_copy(0).start()

    @pl.when(near_above > 0)
    def _():
        pl.semaphore_wait(near_sem, near_above)

    for d in range(1, reach + 1):

        @pl.when(me + d < ne)
        def _():
            green_copy(d).start()

    both = has_above & has_below
    lower_first = lax.rem(layer, 2) == 1
    early = jnp.where(both, jnp.where(lower_first, 0, 1), jnp.where(has_above, 0, 1))
    late = 1 - early

    @pl.when(jnp.logical_not(both))
    def _():
        ps[early] = jnp.zeros(ps.shape[1:], F32)

    for d in range(1, reach + 1):

        @pl.when(me < d)
        def _():
            gin[d - 1] = jnp.zeros((packed, atoms), BF16)

    for slot in range(1, pin.shape[0]):

        @pl.when(jnp.logical_not(heard(slot)))
        def _():
            pin[slot] = jnp.zeros(pin.shape[1:], BF16)

    e16_ref[...] = expansion(order, depth, packed)
    load_coup.wait()
    for t in range(tiles):
        block = coup_ref[:, :, t * LANES : (t + 1) * LANES].astype(F32)
        block = block.reshape(order, order, nbr, LANES)
        c4[:, :, t * size : (t + 1) * size, :] = block[:, :, slots[0] :, :]
        for side in range(2):
            for n in range(2):
                at = n * tiles + t
                cx[side, :, :, at : at + 1, :] = block[:, :, side : side + 1, :]
    lower = lax.broadcasted_iota(jnp.int32, (order, fold, LANES), 1) < tiles
    for side in range(2):
        for i in range(0, order, 2):
            cp[side, i // 2] = jnp.where(lower, cx[side, i], cx[side, i + 1])

    last = off[-1] + 1
    pscr[last * pad :, :] = jnp.zeros(((packed - last) * pad, LANES), F32)
    for side in range(2):
        ps[side, last * fold :, :] = jnp.zeros(((packed - last) * fold, LANES), F32)

    def entries(p, rows):
        at = [off[min(p, q)] + abs(p - q) for q in range(order)]
        return [slice(a * rows, (a + 1) * rows) for a in at]

    def products():
        for i in range(0, order, 2):
            first = jnp.zeros((2, order, pad, LANES), F32)
            for p in range(order):
                block = jnp.stack([g3[at, :] for at in entries(p, pad)])
                first = first + c4[i : i + 2, p][:, None] * block[None]
            total = first[:, 0][:, None] * c4[i:, 0][None]
            for q in range(1, order):
                total = total + first[:, q][:, None] * c4[i:, q][None]
            total = total.astype(BF16).astype(F32)
            for n in range(2):
                pscr[off[i + n] * pad : (off[i + n] + order - i - n) * pad, :] = total[
                    n, n:
                ].reshape(-1, LANES)

    def side_products(side, start, stop):
        for i in range(start, stop, 2):
            first = jnp.zeros((order, fold, LANES), F32)
            for p in range(order):
                block = jnp.stack([gs[side, at, :] for at in entries(p, fold)])
                first = first + cp[side, i // 2, p][None] * block
            total = first[0][None] * cx[side, i:, 0]
            for q in range(1, order):
                total = total + first[q][None] * cx[side, i:, q]
            total = total.astype(BF16).astype(F32).reshape(-1, LANES)
            ps[side, off[i] * fold : off[i + 1] * fold, :] = total
            second = total[fold:].reshape(-1, fold, LANES)
            second = jnp.concatenate([second[:, tiles:], second[:, :tiles]], axis=1)
            ps[side, off[i + 1] * fold : (off[i + 1] + order - i - 1) * fold, :] = second.reshape(
                -1, LANES
            )

    products()

    load_weight.wait()
    load_shift.wait()

    def add_weights(w, sums):
        shift = shift_ref[w]
        low, high = weight_ref[w], weight_ref[freqs + w]
        new = []
        for d in range(1, reach + 1):
            pick = jnp.where(shift == d, 1.0, 0.0).astype(F32)
            new += [sums[2 * d - 2] + pick * low, sums[2 * d - 1] + pick * high]
        return tuple(new)

    sums = lax.fori_loop(
        0, freqs, add_weights, tuple(jnp.zeros((nbr, atoms), F32) for _ in range(2 * reach)),
        unroll=4,
    )
    for s in range(2 * reach):
        ab[s] = sums[s]
        for side in range(2):
            aw[side, s] = jnp.broadcast_to(sums[s][side : side + 1], aw.shape[2:])

    def rows_of(j, t, start, stop):
        at = start * pad + t * size + j
        return pscr[pl.ds(at, stop - start, stride=pad), :]

    def side_rows(side, t, start, stop):
        return ps[side, pl.ds(start * fold + t, stop - start, stride=fold), :]

    def side_partials(side, t, s, start, stop):
        lanes = slice(t * LANES, (t + 1) * LANES)
        weight = aw[side, s, 0:1, lanes]
        return pacc[s, start:stop, lanes] + weight * side_rows(side, t, start, stop)

    for t in range(tiles):
        lanes = slice(t * LANES, (t + 1) * LANES)
        for s in range(2 * reach):
            total = None
            for j, k in enumerate(slots):
                term = ab[s, k : k + 1, lanes] * rows_of(j, t, 0, packed)
                total = term if total is None else total + term
            pacc[s, :, lanes] = total

    g16[...] = jnp.zeros_like(g16)
    for p in range(order):
        g16[p, :order, :] = green_ref[p].astype(F32)
    sig_ref[...] = jnp.zeros_like(sig_ref)

    @pl.when(both & lower_first)
    def _():
        halo_copy(0).wait_recv()

    @pl.when(both & jnp.logical_not(lower_first))
    def _():
        halo_copy(1).wait_recv()

    @pl.when(both)
    def _():
        pick_side(early)
        side_products(early, 0, order)
        for t in range(tiles):
            for s in range(2 * reach):
                pacc[s, :, t * LANES : (t + 1) * LANES] = side_partials(early, t, s, 0, packed)

    @pl.when(late == 0)
    def _():
        halo_copy(0).wait_recv()

    @pl.when(late == 1)
    def _():
        halo_copy(1).wait_recv()

    pick_side(late)

    def correlations():
        @pl.when(far_above > 0)
        def _():
            pl.semaphore_wait(far_sem, far_above)

        wait_gin()

        index = lax.broadcasted_iota(jnp.int32, (packed, LANES), 0)
        twice = jnp.full((packed, LANES), 2.0, F32)
        for p in range(order):
            twice = jnp.where(index == off[p], 1.0, twice)
        rows = [[None] * tiles for _ in range(reach * nbr)]

        for t in range(tiles):
            greens = [
                gin[d, :, t * LANES : (t + 1) * LANES].astype(F32) * twice for d in range(reach)
            ]
            for k in range(nbr):
                if k < 2:
                    value = side_rows(k, t, 0, packed)
                else:
                    value = rows_of(k - 2, t, 0, packed)
                for d in range(reach):
                    rows[d * nbr + k][t] = jnp.sum(greens[d] * value, axis=0, keepdims=True)

        sums = [jnp.concatenate([r[t] for r in rows], axis=0) for t in range(tiles)]
        lane = lax.broadcasted_iota(jnp.int32, sums[0].shape, 1)
        for e in range(ne):
            start = e * share % LANES
            low, high = e * share // LANES, (e * share + share - 1) // LANES
            chunks[e] = sums[low] if low == high else jnp.where(lane >= start, sums[low], sums[high])
        for r in range(1, ne):
            chunk_copy(r).start()

    for n, (start, stop, first, final) in enumerate(plan):
        if first < final:
            side_products(late, first, final)
            if final == order:
                pl.when(me >= ne // 2)(correlations)
        for t in range(tiles):
            lanes = slice(t * LANES, (t + 1) * LANES)
            for s in range(2 * reach):
                pout[s, start:stop, lanes] = side_partials(late, t, s, start, stop).astype(BF16)

        @pl.when(even)
        def _():
            for e, slot in straight[0]:

                @pl.when(reaches(me + e))
                def _():
                    part_copy(outgoing(e), pin.at[slot], n, e).start()

            for number, (e, _) in enumerate(shared):

                @pl.when(reaches(me + e))
                def _():
                    share_copy(outgoing(e), number, n).start()

            part_copy(outgoing(1), pin.at[0], n, 1).start()

        @pl.when(odd)
        def _():
            for e, slot in straight[1]:

                @pl.when(reaches(me + e))
                def _():
                    part_copy(outgoing(e), pin.at[slot], n, e).start()

            part_copy(outgoing(-1), pin.at[0], n, -1).start()

    pl.when(me < ne // 2)(correlations)

    @pl.when(odd)
    def _():
        for n, (start, stop, _, _) in enumerate(plan):
            wait_shared(pl.ds(start, stop - start), n)
            for number, (e, slot) in enumerate(shared):
                out = outgoing(e - 1)

                @pl.when(reaches(base + e))
                def _():
                    for t in range(tiles):
                        lanes = slice(t * LANES, (t + 1) * LANES)
                        total = side_partials(late, t, out, start, stop)
                        total = total + given[number, start:stop, lanes].astype(F32)
                        pout[out, start:stop, lanes] = total.astype(BF16)
                    part_copy(out, pin.at[slot], n, e - 1).start()

    for n, (start, stop, _, _) in enumerate(plan):
        first, final = complete(order, start), complete(order, stop)
        wait_heard(pl.ds(start, stop - start), n)
        sigma = pin[0, start:stop].astype(F32)
        for s in range(1, pin.shape[0]):
            sigma = sigma + pin[s, start:stop].astype(F32)
        sig_ref[start:stop, :] = sigma.astype(BF16)
        s16[first:final] = jnp.dot(
            e16_ref[first * depth : final * depth, :], sig_ref[...], preferred_element_type=F32
        ).reshape(final - first, depth, atoms)
        for i in range(0, order, 2):
            left = [None if first == 0 else l16[i + m] for m in range(2)]
            for p in range(first, final):
                block = s16[p]
                for m in range(2):
                    term = g16[i + m, p : p + 1, :] * block
                    left[m] = term if left[m] is None else left[m] + term
            for m in range(2):
                l16[i + m] = left[m].astype(BF16).astype(F32) if stop == packed else left[m]

    for i in range(0, order, 2):
        total = [g16[i + n] for n in range(2)]
        for p in range(order):
            block = g16[p]
            total = [total[n] + l16[i + n, p : p + 1, :] * block for n in range(2)]
        for n in range(2):
            cor_ref[i + n] = total[n][:order].astype(BF16)

    wait_chunks().wait_recv()
    summed = chunks[me]
    for r in range(1, ne):
        summed = summed + cin[r]
    summed = pltpu.roll(summed, lax.rem(ne * LANES - me * share, LANES), 1)
    summed = summed[:, :share] * (1.0 / (order * math.sqrt(ne)))
    for w in range(freqs):
        shift = shift_ref[w]
        value = jnp.zeros((nbr, share), F32)
        for d in range(1, reach + 1):
            value = jnp.where(shift == d, summed[(d - 1) * nbr : d * nbr], value)
        pol_ref[w] = value

    wait_sent()
    wait_chunks().wait_send()


def finish(cor_ref, pol_ref, cor_hbm, pol_hbm, sem):
    first = pltpu.make_async_copy(cor_ref, cor_hbm, sem.at[0])
    second = pltpu.make_async_copy(pol_ref, pol_hbm, sem.at[1])
    first.start()
    second.start()
    first.wait()
    second.wait()


def body(green_blocks, coupling, phonon_weights, neighbours, phonon_shifts):
    ne = lax.axis_size("energy")
    reach = max(ne // 4, 1)
    order = green_blocks.shape[1]
    atoms = green_blocks.shape[3]
    nbr = neighbours.shape[0]
    freqs = phonon_shifts.shape[0]
    tiles = atoms // LANES
    share = atoms // ne
    count = order * (order + 1) // 2
    packed = -(-count // 16) * 16
    pad = -(-(tiles * (nbr - 2)) // 8) * 8
    fold = -(-(2 * tiles) // 8) * 8
    rows = 16 * (-(-order // 16))
    parts = len(segments(order, packed))
    vmem = pl.BlockSpec(memory_space=pltpu.VMEM)
    hbm = pl.BlockSpec(memory_space=pltpu.HBM)
    dma = pltpu.SemaphoreType.DMA
    green = green_blocks[0]
    staged = pl.pallas_call(
        functools.partial(kernel, reach),
        out_shape=(
            jax.ShapeDtypeStruct((order, order, atoms), BF16),
            jax.ShapeDtypeStruct((freqs, nbr, share), F32),
        ),
        in_specs=[hbm] * 5,
        out_specs=(vmem, vmem),
        scratch_shapes=[
            pltpu.SMEM((freqs,), jnp.int32),
            pltpu.VMEM((order, order, atoms), BF16),
            pltpu.VMEM((order * order, nbr, atoms), BF16),
            pltpu.VMEM((2 * freqs, nbr, atoms), F32),
            pltpu.VMEM((nbr, atoms), jnp.int32),
            pltpu.VMEM((order * rows, packed), BF16),
            pltpu.VMEM((packed, atoms), BF16),
            pltpu.VMEM((order, rows, atoms), F32),
            pltpu.VMEM((order, rows, atoms), F32),
            pltpu.VMEM((order, rows, atoms), F32),
            pltpu.VMEM((packed, atoms), F32),
            pltpu.VMEM((packed, atoms), BF16),
            pltpu.VMEM((2, packed, atoms), BF16),
            pltpu.VMEM((reach, packed, atoms), BF16),
            pltpu.VMEM((2 * reach, packed, atoms), BF16),
            pltpu.VMEM((1 + 2 * ((reach + 1) // 2), packed, atoms), BF16),
            pltpu.VMEM((max(len(routes(reach)[1]), 1), packed, atoms), BF16),
            pltpu.VMEM((4 + 3 * reach, packed, atoms), BF16),
            pltpu.VMEM((2 * reach, packed, atoms), F32),
            pltpu.VMEM((2, atoms, atoms), BF16),
            pltpu.VMEM((ne, reach * nbr, LANES), F32),
            pltpu.VMEM((ne, reach * nbr, LANES), F32),
            pltpu.VMEM((order, order, pad, LANES), F32),
            pltpu.VMEM((packed * pad, LANES), F32),
            pltpu.VMEM((packed * pad, LANES), F32),
            pltpu.VMEM((2, order, order, fold, LANES), F32),
            pltpu.VMEM((2, order // 2, order, fold, LANES), F32),
            pltpu.VMEM((2, packed * fold, LANES), F32),
            pltpu.VMEM((2, packed * fold, LANES), F32),
            pltpu.VMEM((2 * reach, nbr, atoms), F32),
            pltpu.VMEM((2, 2 * reach, 8, atoms), F32),
            dma((3,)), *[pltpu.SemaphoreType.REGULAR] * 3,
            dma((1,)), dma((2,)), dma((1,)), dma((parts,)), dma((parts,)), dma((1,)), dma((1,)),
        ],
        compiler_params=pltpu.CompilerParams(
            collective_id=0, has_side_effects=True, vmem_limit_bytes=VMEM_LIMIT
        ),
    )(
        *(
            pltpu.with_memory_space_constraint(x, pltpu.HBM)
            for x in (
                phonon_shifts,
                green,
                coupling.reshape(order * order, nbr, atoms),
                phonon_weights.reshape(2 * freqs, nbr, atoms),
                neighbours,
            )
        )
    )
    corrected, polarization = pl.pallas_call(
        finish,
        out_shape=(
            jax.ShapeDtypeStruct((order, order, atoms), BF16),
            jax.ShapeDtypeStruct((freqs, nbr, share), F32),
        ),
        in_specs=[vmem, vmem],
        out_specs=(hbm, hbm),
        scratch_shapes=[dma((2,))],
        compiler_params=pltpu.CompilerParams(vmem_limit_bytes=VMEM_LIMIT),
    )(*staged)
    return corrected[None], polarization


def solution(mesh):
    return jax.shard_map(
        body,
        mesh=mesh,
        in_specs=(
            P("energy", None, None, "layer"),
            P(None, None, None, "layer"),
            P(None, None, None, "layer"),
            P(None, "layer"),
            P(),
        ),
        out_specs=(P("energy", None, None, "layer"), P(None, None, ("layer", "energy"))),
        check_vma=False,
    )
```

```python
import functools
import math

import jax
import jax.numpy as jnp
from jax import lax
from jax.experimental import pallas as pl
from jax.experimental.pallas import tpu as pltpu
from jax.sharding import PartitionSpec as P

MESH = pl.DeviceIdType.MESH
LANES = 128
F32 = jnp.float32
BF16 = jnp.bfloat16
VMEM_LIMIT = 48 * 1024 * 1024


def offsets(order):
    return [p * order - p * (p - 1) // 2 for p in range(order)]


def segments(order, packed):
    stops = [16] + [o // 16 * 16 for o in offsets(order)[8::4]] + [packed]
    plan, start, first = [], 0, 0
    for stop in stops:
        if stop > start:
            final = 2 if start == 0 else order
            plan.append((start, stop, first, final))
            start, first = stop, final
    return plan


def routes(reach):
    straight, shared = ([], []), []
    for d in range(1, (reach + 1) // 2 + 1):
        for way in (1, -1):
            slot = 2 * d - (way > 0)
            for parity in range(2):
                far = [abs(2 * d * way + parity - p) for p in range(2)]
                near = [p for p in range(2) if far[p] <= reach]
                if len(near) == 2:
                    shared.append((2 * d * way + parity, slot))
                elif near:
                    straight[near[0]].append((2 * d * way + parity - near[0], slot))
    return straight, shared


def complete(order, stop):
    return sum(o + order - p <= stop for p, o in enumerate(offsets(order)))


def expansion(order, row_stride, packed_rows):
    row = lax.broadcasted_iota(jnp.int32, (order * row_stride, packed_rows), 0)
    column = lax.broadcasted_iota(jnp.int32, (order * row_stride, packed_rows), 1)
    p, q = row // row_stride, row % row_stride
    low, high = jnp.minimum(p, q), jnp.maximum(p, q)
    entry = low * order - low * (low - 1) // 2 + high - low
    return jnp.where((entry == column) & (q < order), 1.0, 0.0).astype(BF16)


def kernel(
    reach, shift_hbm, green_hbm, coup_hbm, weight_hbm, near_hbm, cor_ref, pol_ref,
    shift_ref, green_ref, coup_ref, weight_ref, near_ref, e16_ref, sig_ref,
    g16, s16, l16, tri32, own, halo, gin, pout, pin, given, landing, pacc, hots, chunks, cin, c4, g3, pscr, cx, cp, gs, ps, ab, aw,
    load_sem, side_sem, near_sem, far_sem, sent_sem, halo_recv, gin_recv, part_recv, share_recv,
    chunk_send, chunk_recv,
):
    order = green_ref.shape[0]
    atoms = green_ref.shape[2]
    nbr = near_ref.shape[0]
    freqs = shift_ref.shape[0]
    tiles = atoms // LANES
    packed = own.shape[0]
    pad = c4.shape[2]
    fold = cx.shape[3]
    ne = lax.axis_size("energy")
    nl = lax.axis_size("layer")
    me = lax.axis_index("energy")
    layer = lax.axis_index("layer")
    share = atoms // ne
    depth = s16.shape[1]
    off = offsets(order)
    plan = segments(order, packed)
    slots = tuple(range(2, nbr))
    size = len(slots)

    def load(n, src, dst):
        copy = pltpu.make_async_copy(src, dst, load_sem.at[n])
        copy.start()
        return copy

    step = order // 4
    for p in range(0, order, step):
        load(0, green_hbm.at[pl.ds(p, step)], green_ref.at[pl.ds(p, step)])
    load_green = pltpu.make_async_copy(green_hbm, green_ref, load_sem.at[0])
    load_near = load(1, near_hbm, near_ref)
    load_shift = load(2, shift_hbm, shift_ref)

    barrier = pltpu.get_barrier_semaphore()

    def greet(sem, energy, row):
        pl.semaphore_signal(
            sem, inc=1, device_id={"energy": energy, "layer": row}, device_id_type=MESH
        )

    odd = lax.rem(me, 2) == 1
    even = jnp.logical_not(odd)
    relayed = me >= ne - 2
    told = even & relayed
    has_above, has_below = layer < nl - 1, layer > 0
    near_above = jnp.minimum(ne - 1 - me, reach)
    near_count = near_above + jnp.minimum(me, reach)
    far_above = ne - 1 - me - near_above

    @pl.when(has_below)
    def _():
        greet(barrier, me + told.astype(jnp.int32), layer - 1)

    @pl.when(odd)
    def _():
        greet(barrier, me - 1, layer)

    @pl.when(has_above)
    def _():
        greet(barrier, me, layer + 1)

    for d in range(1, ne):

        @pl.when(me + d < ne)
        def _():
            greet(barrier, me + d, layer)

    tri32[...] = jnp.zeros_like(tri32)
    load_green.wait()
    load_coup = load(0, coup_hbm, coup_ref)
    for p in range(order):
        tri32[off[p] : off[p] + order - p, :] = green_ref[p].astype(F32)[p:, :]
    own[...] = tri32[...].astype(BF16)

    pl.semaphore_wait(
        barrier,
        me
        + even.astype(jnp.int32)
        + has_below.astype(jnp.int32)
        + jnp.where(told, 0, jnp.where(relayed, 2, 1)) * has_above.astype(jnp.int32),
    )

    def remote(src, dst, send, recv, energy, row):
        return pltpu.make_async_remote_copy(
            src_ref=src, dst_ref=dst, send_sem=send, recv_sem=recv,
            device_id={"energy": energy, "layer": row}, device_id_type=MESH,
        )

    straight, shared = routes(reach)
    base = me - lax.rem(me, 2)

    def reaches(offset):
        return (offset >= 0) & (offset < ne)

    def heard(slot):
        d = (slot + 1) // 2
        if slot % 2:
            return (base >= 2 * d) & (2 * d - even.astype(jnp.int32) <= reach)
        return (base + 2 * d < ne) & (2 * d - odd.astype(jnp.int32) <= reach)

    def number(conditions):
        total = 0
        for condition in conditions:
            total = total + condition.astype(jnp.int32)
        return total

    heard_count = 1 + number([heard(slot) for slot in range(1, pin.shape[0])])
    shared_count = number([reaches(base + e) for e, _ in shared])
    sent_count = 1 + shared_count + near_above + number([has_above, has_below])
    for parity in range(2):
        which = odd if parity else even
        sent_count = sent_count + number([which & reaches(me + e) for e, _ in straight[parity]])

    def halo_copy(side):
        row = layer + 1 if side == 0 else layer - 1
        return remote(own, halo.at[side], sent_sem.at[0], halo_recv.at[side], me, row)

    def green_copy(d):
        return remote(
            own, gin.at[d - 1], sent_sem.at[0], gin_recv.at[0], me + d, layer
        )

    arrivals = [(0, plan[1][1])] + [(start, stop) for start, stop, _, _ in plan[2:]]

    def group(start):
        return sum(start >= stop for _, stop in arrivals)

    def part_copy(source, target, start, stop, e):
        rows = pl.ds(start, stop - start)
        return remote(
            pout.at[source, rows], target.at[rows], sent_sem.at[0],
            part_recv.at[group(start)], me + e, layer,
        )

    def share_copy(source, number, start, stop):
        rows = pl.ds(start, stop - start)
        return remote(
            pout.at[source, rows], given.at[number, rows], sent_sem.at[0], share_recv.at[group(start)],
            me + 1, layer,
        )

    def outgoing(offset):
        return 2 * offset - 2 if offset > 0 else -2 * offset - 1

    def chunk_copy(r):
        dest = lax.rem(me + r, ne)
        return remote(
            chunks.at[dest], cin.at[r], chunk_send.at[0], chunk_recv.at[0], dest, layer
        )

    def wait_gin():
        for c in range(1, reach + 1):

            @pl.when(jnp.minimum(me, reach) == c)
            def _():
                some = gin.at[pl.ds(0, c)]
                remote(some, some, sent_sem.at[0], gin_recv.at[0], me, layer).wait_recv()

    def wait_parts(count, most, rows, copy_of):
        for c in range(1, most + 1):

            @pl.when(count == c)
            def _():
                copy_of(landing.at[pl.ds(0, c), rows])

    def wait_heard(rows, n):
        wait_parts(
            heard_count, pin.shape[0], rows,
            lambda some: remote(
                some, some, sent_sem.at[0], part_recv.at[n], me, layer
            ).wait_recv(),
        )

    def wait_shared(rows, n):
        wait_parts(
            shared_count, len(shared), rows,
            lambda some: remote(
                some, some, sent_sem.at[0], share_recv.at[n], me, layer
            ).wait_recv(),
        )

    def wait_sent():
        wait_parts(
            sent_count, landing.shape[0], pl.ds(0, packed),
            lambda some: remote(
                some, some, sent_sem.at[0], part_recv.at[0], me, layer
            ).wait_send(),
        )

    def wait_chunks():
        some = cin.at[pl.ds(1, ne - 1)]
        return remote(some, some, chunk_send.at[0], chunk_recv.at[0], me, layer)

    @pl.when(has_below)
    def _():
        halo_copy(1).start()

    @pl.when(has_above & jnp.logical_not(told))
    def _():
        halo_copy(0).start()

    @pl.when(has_above & odd & relayed)
    def _():
        greet(side_sem, me - 1, layer)

    for d in range(1, ne):

        @pl.when(me >= d)
        def _():
            greet(near_sem if d <= reach else far_sem, me - d, layer)

    row = lax.broadcasted_iota(jnp.int32, (atoms, atoms), 0)

    def one_hot(k, start):
        return jnp.where(row == near_ref[k : k + 1, :] - start, 1.0, 0.0).astype(BF16)

    def taken(blocks, hot):
        found = jnp.dot(blocks, hot, preferred_element_type=F32)
        return [found[:, t * LANES : (t + 1) * LANES] for t in range(tiles)]

    def pick_side(side):
        for t, found in enumerate(taken(halo[side], hots[side])):
            for n in range(2):
                gs[side, pl.ds(n * tiles + t, packed, stride=fold), :] = found

    load_near.wait()
    load_weight = load(1, weight_hbm, weight_ref)
    for j, k in enumerate(slots):
        for t, found in enumerate(taken(own[...], one_hot(k, atoms))):
            g3[pl.ds(t * size + j, packed, stride=pad), :] = found
    hots[0] = one_hot(0, 0)
    hots[1] = one_hot(1, 2 * atoms)

    @pl.when(told & has_above)
    def _():
        pl.semaphore_wait(side_sem, 1)
        halo_copy(0).start()

    @pl.when(near_above > 0)
    def _():
        pl.semaphore_wait(near_sem, near_above)

    for d in range(1, reach + 1):

        @pl.when(me + d < ne)
        def _():
            green_copy(d).start()

    both = has_above & has_below
    lower_first = lax.rem(layer, 2) == 1
    early = jnp.where(both, jnp.where(lower_first, 0, 1), jnp.where(has_above, 0, 1))
    late = 1 - early

    @pl.when(jnp.logical_not(both))
    def _():
        ps[early] = jnp.zeros(ps.shape[1:], F32)

    for d in range(1, reach + 1):

        @pl.when(me < d)
        def _():
            gin[d - 1] = jnp.zeros((packed, atoms), BF16)

    for slot in range(1, pin.shape[0]):

        @pl.when(jnp.logical_not(heard(slot)))
        def _():
            pin[slot] = jnp.zeros(pin.shape[1:], BF16)

    e16_ref[...] = expansion(order, depth, packed)
    load_coup.wait()
    for t in range(tiles):
        block = coup_ref[:, :, t * LANES : (t + 1) * LANES].astype(F32)
        block = block.reshape(order, order, nbr, LANES)
        c4[:, :, t * size : (t + 1) * size, :] = block[:, :, slots[0] :, :]
        for side in range(2):
            for n in range(2):
                at = n * tiles + t
                cx[side, :, :, at : at + 1, :] = block[:, :, side : side + 1, :]
    lower = lax.broadcasted_iota(jnp.int32, (order, fold, LANES), 1) < tiles
    for side in range(2):
        for i in range(0, order, 2):
            cp[side, i // 2] = jnp.where(lower, cx[side, i], cx[side, i + 1])

    last = off[-1] + 1
    pscr[last * pad :, :] = jnp.zeros(((packed - last) * pad, LANES), F32)
    for side in range(2):
        ps[side, last * fold :, :] = jnp.zeros(((packed - last) * fold, LANES), F32)

    def entries(p, rows):
        at = [off[min(p, q)] + abs(p - q) for q in range(order)]
        return [slice(a * rows, (a + 1) * rows) for a in at]

    def products():
        for i in range(0, order, 2):
            first = jnp.zeros((2, order, pad, LANES), F32)
            for p in range(order):
                block = jnp.stack([g3[at, :] for at in entries(p, pad)])
                first = first + c4[i : i + 2, p][:, None] * block[None]
            total = first[:, 0][:, None] * c4[i:, 0][None]
            for q in range(1, order):
                total = total + first[:, q][:, None] * c4[i:, q][None]
            total = total.astype(BF16).astype(F32)
            for n in range(2):
                pscr[off[i + n] * pad : (off[i + n] + order - i - n) * pad, :] = total[
                    n, n:
                ].reshape(-1, LANES)

    def side_products(side, start, stop):
        for i in range(start, stop, 2):
            first = jnp.zeros((order, fold, LANES), F32)
            for p in range(order):
                block = jnp.stack([gs[side, at, :] for at in entries(p, fold)])
                first = first + cp[side, i // 2, p][None] * block
            total = first[0][None] * cx[side, i:, 0]
            for q in range(1, order):
                total = total + first[q][None] * cx[side, i:, q]
            total = total.astype(BF16).astype(F32).reshape(-1, LANES)
            ps[side, off[i] * fold : off[i + 1] * fold, :] = total
            second = total[fold:].reshape(-1, fold, LANES)
            second = jnp.concatenate([second[:, tiles:], second[:, :tiles]], axis=1)
            ps[side, off[i + 1] * fold : (off[i + 1] + order - i - 1) * fold, :] = second.reshape(
                -1, LANES
            )

    products()

    load_weight.wait()
    load_shift.wait()

    def add_weights(w, sums):
        shift = shift_ref[w]
        low, high = weight_ref[w], weight_ref[freqs + w]
        new = []
        for d in range(1, reach + 1):
            pick = jnp.where(shift == d, 1.0, 0.0).astype(F32)
            new += [sums[2 * d - 2] + pick * low, sums[2 * d - 1] + pick * high]
        return tuple(new)

    sums = lax.fori_loop(
        0, freqs, add_weights, tuple(jnp.zeros((nbr, atoms), F32) for _ in range(2 * reach)),
        unroll=4,
    )
    for s in range(2 * reach):
        ab[s] = sums[s]
        for side in range(2):
            aw[side, s] = jnp.broadcast_to(sums[s][side : side + 1], aw.shape[2:])

    def rows_of(j, t, start, stop):
        at = start * pad + t * size + j
        return pscr[pl.ds(at, stop - start, stride=pad), :]

    def side_rows(side, t, start, stop):
        return ps[side, pl.ds(start * fold + t, stop - start, stride=fold), :]

    def side_partials(side, t, s, start, stop):
        lanes = slice(t * LANES, (t + 1) * LANES)
        weight = aw[side, s, 0:1, lanes]
        return pacc[s, start:stop, lanes] + weight * side_rows(side, t, start, stop)

    for t in range(tiles):
        lanes = slice(t * LANES, (t + 1) * LANES)
        for s in range(2 * reach):
            total = None
            for j, k in enumerate(slots):
                term = ab[s, k : k + 1, lanes] * rows_of(j, t, 0, packed)
                total = term if total is None else total + term
            pacc[s, :, lanes] = total

    g16[...] = jnp.zeros_like(g16)
    for p in range(order):
        g16[p, :order, :] = green_ref[p].astype(F32)
    sig_ref[...] = jnp.zeros_like(sig_ref)

    @pl.when(both & lower_first)
    def _():
        halo_copy(0).wait_recv()

    @pl.when(both & jnp.logical_not(lower_first))
    def _():
        halo_copy(1).wait_recv()

    @pl.when(both)
    def _():
        pick_side(early)
        side_products(early, 0, order)
        for t in range(tiles):
            for s in range(2 * reach):
                pacc[s, :, t * LANES : (t + 1) * LANES] = side_partials(early, t, s, 0, packed)

    @pl.when(late == 0)
    def _():
        halo_copy(0).wait_recv()

    @pl.when(late == 1)
    def _():
        halo_copy(1).wait_recv()

    pick_side(late)

    def correlations():
        @pl.when(far_above > 0)
        def _():
            pl.semaphore_wait(far_sem, far_above)

        wait_gin()

        index = lax.broadcasted_iota(jnp.int32, (packed, LANES), 0)
        twice = jnp.full((packed, LANES), 2.0, F32)
        for p in range(order):
            twice = jnp.where(index == off[p], 1.0, twice)
        rows = [[None] * tiles for _ in range(reach * nbr)]

        for t in range(tiles):
            greens = [
                gin[d, :, t * LANES : (t + 1) * LANES].astype(F32) * twice for d in range(reach)
            ]
            for k in range(nbr):
                if k < 2:
                    value = side_rows(k, t, 0, packed)
                else:
                    value = rows_of(k - 2, t, 0, packed)
                for d in range(reach):
                    rows[d * nbr + k][t] = jnp.sum(greens[d] * value, axis=0, keepdims=True)

        sums = [jnp.concatenate([r[t] for r in rows], axis=0) for t in range(tiles)]
        lane = lax.broadcasted_iota(jnp.int32, sums[0].shape, 1)
        for e in range(ne):
            start = e * share % LANES
            low, high = e * share // LANES, (e * share + share - 1) // LANES
            chunks[e] = sums[low] if low == high else jnp.where(lane >= start, sums[low], sums[high])
        for r in range(1, ne):
            chunk_copy(r).start()

    for n, (start, stop, first, final) in enumerate(plan):
        if first < final:
            side_products(late, first, final)
            if final == order:
                pl.when(me >= ne // 2)(correlations)
        for t in range(tiles):
            lanes = slice(t * LANES, (t + 1) * LANES)
            for s in range(2 * reach):
                pout[s, start:stop, lanes] = side_partials(late, t, s, start, stop).astype(BF16)

        @pl.when(even)
        def _():
            for e, slot in straight[0]:

                @pl.when(reaches(me + e))
                def _():
                    part_copy(outgoing(e), pin.at[slot], start, stop, e).start()

            for number, (e, _) in enumerate(shared):

                @pl.when(reaches(me + e))
                def _():
                    share_copy(outgoing(e), number, start, stop).start()

            part_copy(outgoing(1), pin.at[0], start, stop, 1).start()

        @pl.when(odd)
        def _():
            for e, slot in straight[1]:

                @pl.when(reaches(me + e))
                def _():
                    part_copy(outgoing(e), pin.at[slot], start, stop, e).start()

            part_copy(outgoing(-1), pin.at[0], start, stop, -1).start()

    pl.when(me < ne // 2)(correlations)

    @pl.when(odd)
    def _():
        for n, (start, stop) in enumerate(arrivals):
            wait_shared(pl.ds(start, stop - start), n)
            for number, (e, slot) in enumerate(shared):
                out = outgoing(e - 1)

                @pl.when(reaches(base + e))
                def _():
                    for t in range(tiles):
                        lanes = slice(t * LANES, (t + 1) * LANES)
                        total = side_partials(late, t, out, start, stop)
                        total = total + given[number, start:stop, lanes].astype(F32)
                        pout[out, start:stop, lanes] = total.astype(BF16)
                    part_copy(out, pin.at[slot], start, stop, e - 1).start()

    for n, (start, stop) in enumerate(arrivals):
        first, final = complete(order, start), complete(order, stop)
        wait_heard(pl.ds(start, stop - start), n)
        sigma = pin[0, start:stop].astype(F32)
        for s in range(1, pin.shape[0]):
            sigma = sigma + pin[s, start:stop].astype(F32)
        sig_ref[start:stop, :] = sigma.astype(BF16)
        s16[first:final] = jnp.dot(
            e16_ref[first * depth : final * depth, :], sig_ref[...], preferred_element_type=F32
        ).reshape(final - first, depth, atoms)
        for i in range(0, order, 2):
            left = [None if first == 0 else l16[i + m] for m in range(2)]
            for p in range(first, final):
                block = s16[p]
                for m in range(2):
                    term = g16[i + m, p : p + 1, :] * block
                    left[m] = term if left[m] is None else left[m] + term
            for m in range(2):
                l16[i + m] = left[m].astype(BF16).astype(F32) if stop == packed else left[m]

    for i in range(0, order, 2):
        total = [g16[i + n] for n in range(2)]
        for p in range(order):
            block = g16[p]
            total = [total[n] + l16[i + n, p : p + 1, :] * block for n in range(2)]
        for n in range(2):
            cor_ref[i + n] = total[n][:order].astype(BF16)

    wait_chunks().wait_recv()
    summed = chunks[me]
    for r in range(1, ne):
        summed = summed + cin[r]
    summed = pltpu.roll(summed, lax.rem(ne * LANES - me * share, LANES), 1)
    summed = summed[:, :share] * (1.0 / (order * math.sqrt(ne)))
    for w in range(freqs):
        shift = shift_ref[w]
        value = jnp.zeros((nbr, share), F32)
        for d in range(1, reach + 1):
            value = jnp.where(shift == d, summed[(d - 1) * nbr : d * nbr], value)
        pol_ref[w] = value

    wait_sent()
    wait_chunks().wait_send()


def finish(cor_ref, pol_ref, cor_hbm, pol_hbm, sem):
    first = pltpu.make_async_copy(cor_ref, cor_hbm, sem.at[0])
    second = pltpu.make_async_copy(pol_ref, pol_hbm, sem.at[1])
    first.start()
    second.start()
    first.wait()
    second.wait()


def body(green_blocks, coupling, phonon_weights, neighbours, phonon_shifts):
    ne = lax.axis_size("energy")
    reach = max(ne // 4, 1)
    order = green_blocks.shape[1]
    atoms = green_blocks.shape[3]
    nbr = neighbours.shape[0]
    freqs = phonon_shifts.shape[0]
    tiles = atoms // LANES
    share = atoms // ne
    count = order * (order + 1) // 2
    packed = -(-count // 16) * 16
    pad = -(-(tiles * (nbr - 2)) // 8) * 8
    fold = -(-(2 * tiles) // 8) * 8
    rows = 16 * (-(-order // 16))
    parts = len(segments(order, packed)) - 1
    vmem = pl.BlockSpec(memory_space=pltpu.VMEM)
    hbm = pl.BlockSpec(memory_space=pltpu.HBM)
    dma = pltpu.SemaphoreType.DMA
    green = green_blocks[0]
    staged = pl.pallas_call(
        functools.partial(kernel, reach),
        out_shape=(
            jax.ShapeDtypeStruct((order, order, atoms), BF16),
            jax.ShapeDtypeStruct((freqs, nbr, share), F32),
        ),
        in_specs=[hbm] * 5,
        out_specs=(vmem, vmem),
        scratch_shapes=[
            pltpu.SMEM((freqs,), jnp.int32),
            pltpu.VMEM((order, order, atoms), BF16),
            pltpu.VMEM((order * order, nbr, atoms), BF16),
            pltpu.VMEM((2 * freqs, nbr, atoms), F32),
            pltpu.VMEM((nbr, atoms), jnp.int32),
            pltpu.VMEM((order * rows, packed), BF16),
            pltpu.VMEM((packed, atoms), BF16),
            pltpu.VMEM((order, rows, atoms), F32),
            pltpu.VMEM((order, rows, atoms), F32),
            pltpu.VMEM((order, rows, atoms), F32),
            pltpu.VMEM((packed, atoms), F32),
            pltpu.VMEM((packed, atoms), BF16),
            pltpu.VMEM((2, packed, atoms), BF16),
            pltpu.VMEM((reach, packed, atoms), BF16),
            pltpu.VMEM((2 * reach, packed, atoms), BF16),
            pltpu.VMEM((1 + 2 * ((reach + 1) // 2), packed, atoms), BF16),
            pltpu.VMEM((max(len(routes(reach)[1]), 1), packed, atoms), BF16),
            pltpu.VMEM((4 + 3 * reach, packed, atoms), BF16),
            pltpu.VMEM((2 * reach, packed, atoms), F32),
            pltpu.VMEM((2, atoms, atoms), BF16),
            pltpu.VMEM((ne, reach * nbr, LANES), F32),
            pltpu.VMEM((ne, reach * nbr, LANES), F32),
            pltpu.VMEM((order, order, pad, LANES), F32),
            pltpu.VMEM((packed * pad, LANES), F32),
            pltpu.VMEM((packed * pad, LANES), F32),
            pltpu.VMEM((2, order, order, fold, LANES), F32),
            pltpu.VMEM((2, order // 2, order, fold, LANES), F32),
            pltpu.VMEM((2, packed * fold, LANES), F32),
            pltpu.VMEM((2, packed * fold, LANES), F32),
            pltpu.VMEM((2 * reach, nbr, atoms), F32),
            pltpu.VMEM((2, 2 * reach, 8, atoms), F32),
            dma((3,)), *[pltpu.SemaphoreType.REGULAR] * 3,
            dma((1,)), dma((2,)), dma((1,)), dma((parts,)), dma((parts,)), dma((1,)), dma((1,)),
        ],
        compiler_params=pltpu.CompilerParams(
            collective_id=0, has_side_effects=True, vmem_limit_bytes=VMEM_LIMIT
        ),
    )(
        *(
            pltpu.with_memory_space_constraint(x, pltpu.HBM)
            for x in (
                phonon_shifts,
                green,
                coupling.reshape(order * order, nbr, atoms),
                phonon_weights.reshape(2 * freqs, nbr, atoms),
                neighbours,
            )
        )
    )
    corrected, polarization = pl.pallas_call(
        finish,
        out_shape=(
            jax.ShapeDtypeStruct((order, order, atoms), BF16),
            jax.ShapeDtypeStruct((freqs, nbr, share), F32),
        ),
        in_specs=[vmem, vmem],
        out_specs=(hbm, hbm),
        scratch_shapes=[dma((2,))],
        compiler_params=pltpu.CompilerParams(vmem_limit_bytes=VMEM_LIMIT),
    )(*staged)
    return corrected[None], polarization


def solution(mesh):
    return jax.shard_map(
        body,
        mesh=mesh,
        in_specs=(
            P("energy", None, None, "layer"),
            P(None, None, None, "layer"),
            P(None, None, None, "layer"),
            P(None, "layer"),
            P(),
        ),
        out_specs=(P("energy", None, None, "layer"), P(None, None, ("layer", "energy"))),
        check_vma=False,
    )
```

```python
import functools
import math

import jax
import jax.numpy as jnp
from jax import lax
from jax.experimental import pallas as pl
from jax.experimental.pallas import tpu as pltpu
from jax.sharding import PartitionSpec as P

MESH = pl.DeviceIdType.MESH
LANES = 128
F32 = jnp.float32
BF16 = jnp.bfloat16
VMEM_LIMIT = 48 * 1024 * 1024


def offsets(order):
    return [p * order - p * (p - 1) // 2 for p in range(order)]


def segments(order, packed):
    stops = [16] + [o // 16 * 16 for o in offsets(order)[8::4]] + [packed]
    plan, start, first = [], 0, 0
    for stop in stops:
        if stop > start:
            final = 2 if start == 0 else order
            plan.append((start, stop, first, final))
            start, first = stop, final
    return plan


def routes(reach):
    straight, shared = ([], []), []
    for d in range(1, (reach + 1) // 2 + 1):
        for way in (1, -1):
            slot = 2 * d - (way > 0)
            for parity in range(2):
                far = [abs(2 * d * way + parity - p) for p in range(2)]
                near = [p for p in range(2) if far[p] <= reach]
                if len(near) == 2:
                    shared.append((2 * d * way + parity, slot))
                elif near:
                    straight[near[0]].append((2 * d * way + parity - near[0], slot))
    return straight, shared


def complete(order, stop):
    return sum(o + order - p <= stop for p, o in enumerate(offsets(order)))


def expansion(order, row_stride, packed_rows):
    row = lax.broadcasted_iota(jnp.int32, (order * row_stride, packed_rows), 0)
    column = lax.broadcasted_iota(jnp.int32, (order * row_stride, packed_rows), 1)
    p, q = row // row_stride, row % row_stride
    low, high = jnp.minimum(p, q), jnp.maximum(p, q)
    entry = low * order - low * (low - 1) // 2 + high - low
    return jnp.where((entry == column) & (q < order), 1.0, 0.0).astype(BF16)


def kernel(
    reach, shift_hbm, green_hbm, coup_hbm, weight_hbm, near_hbm, cor_ref, pol_ref,
    shift_ref, green_ref, coup_ref, weight_ref, near_ref, e16_ref, sig_ref,
    g16, s16, l16, tri32, own, halo, gin, pout, pin, given, landing, pacc, hots, chunks, cin, c4, g3, pscr, cx, cp, gs, ps, ab, aw,
    load_sem, side_sem, near_sem, far_sem, sent_sem, halo_recv, gin_recv, part_recv, share_recv,
    chunk_send, chunk_recv,
):
    order = green_ref.shape[0]
    atoms = green_ref.shape[2]
    nbr = near_ref.shape[0]
    freqs = shift_ref.shape[0]
    tiles = atoms // LANES
    packed = own.shape[0]
    pad = c4.shape[2]
    fold = cx.shape[3]
    ne = lax.axis_size("energy")
    nl = lax.axis_size("layer")
    me = lax.axis_index("energy")
    layer = lax.axis_index("layer")
    share = atoms // ne
    depth = s16.shape[1]
    off = offsets(order)
    plan = segments(order, packed)
    slots = tuple(range(2, nbr))
    size = len(slots)

    def load(n, src, dst):
        copy = pltpu.make_async_copy(src, dst, load_sem.at[n])
        copy.start()
        return copy

    step = order // 4
    for p in range(0, order, step):
        load(0, green_hbm.at[pl.ds(p, step)], green_ref.at[pl.ds(p, step)])
    load_green = pltpu.make_async_copy(green_hbm, green_ref, load_sem.at[0])
    load_near = load(1, near_hbm, near_ref)

    barrier = pltpu.get_barrier_semaphore()

    def greet(sem, energy, row):
        pl.semaphore_signal(
            sem, inc=1, device_id={"energy": energy, "layer": row}, device_id_type=MESH
        )

    odd = lax.rem(me, 2) == 1
    even = jnp.logical_not(odd)
    relayed = me >= ne - 2
    told = even & relayed
    has_above, has_below = layer < nl - 1, layer > 0
    near_above = jnp.minimum(ne - 1 - me, reach)
    near_count = near_above + jnp.minimum(me, reach)
    far_above = ne - 1 - me - near_above

    @pl.when(has_below)
    def _():
        greet(barrier, me + told.astype(jnp.int32), layer - 1)

    @pl.when(odd)
    def _():
        greet(barrier, me - 1, layer)

    @pl.when(has_above)
    def _():
        greet(barrier, me, layer + 1)

    for d in range(1, ne):

        @pl.when(me + d < ne)
        def _():
            greet(barrier, me + d, layer)

    tri32[...] = jnp.zeros_like(tri32)
    load_green.wait()
    load_coup = load(0, coup_hbm, coup_ref)
    for p in range(order):
        tri32[off[p] : off[p] + order - p, :] = green_ref[p].astype(F32)[p:, :]
    own[...] = tri32[...].astype(BF16)

    pl.semaphore_wait(
        barrier,
        me
        + even.astype(jnp.int32)
        + has_below.astype(jnp.int32)
        + jnp.where(told, 0, jnp.where(relayed, 2, 1)) * has_above.astype(jnp.int32),
    )

    def remote(src, dst, send, recv, energy, row):
        return pltpu.make_async_remote_copy(
            src_ref=src, dst_ref=dst, send_sem=send, recv_sem=recv,
            device_id={"energy": energy, "layer": row}, device_id_type=MESH,
        )

    straight, shared = routes(reach)
    base = me - lax.rem(me, 2)

    def reaches(offset):
        return (offset >= 0) & (offset < ne)

    def heard(slot):
        d = (slot + 1) // 2
        if slot % 2:
            return (base >= 2 * d) & (2 * d - even.astype(jnp.int32) <= reach)
        return (base + 2 * d < ne) & (2 * d - odd.astype(jnp.int32) <= reach)

    def number(conditions):
        total = 0
        for condition in conditions:
            total = total + condition.astype(jnp.int32)
        return total

    heard_count = 1 + number([heard(slot) for slot in range(1, pin.shape[0])])
    shared_count = number([reaches(base + e) for e, _ in shared])
    sent_count = 1 + shared_count + near_above + number([has_above, has_below])
    for parity in range(2):
        which = odd if parity else even
        sent_count = sent_count + number([which & reaches(me + e) for e, _ in straight[parity]])

    def halo_copy(side):
        row = layer + 1 if side == 0 else layer - 1
        return remote(own, halo.at[side], sent_sem.at[0], halo_recv.at[side], me, row)

    def green_copy(d):
        return remote(
            own, gin.at[d - 1], sent_sem.at[0], gin_recv.at[0], me + d, layer
        )

    arrivals = [(0, plan[1][1])] + [(start, stop) for start, stop, _, _ in plan[2:]]

    def group(start):
        return sum(start >= stop for _, stop in arrivals)

    def part_copy(source, target, start, stop, e):
        rows = pl.ds(start, stop - start)
        return remote(
            pout.at[source, rows], target.at[rows], sent_sem.at[0],
            part_recv.at[group(start)], me + e, layer,
        )

    def share_copy(source, number, start, stop):
        rows = pl.ds(start, stop - start)
        return remote(
            pout.at[source, rows], given.at[number, rows], sent_sem.at[0], share_recv.at[group(start)],
            me + 1, layer,
        )

    def outgoing(offset):
        return 2 * offset - 2 if offset > 0 else -2 * offset - 1

    def chunk_copy(r):
        dest = lax.rem(me + r, ne)
        return remote(
            chunks.at[dest], cin.at[r], chunk_send.at[0], chunk_recv.at[0], dest, layer
        )

    def wait_gin():
        for c in range(1, reach + 1):

            @pl.when(jnp.minimum(me, reach) == c)
            def _():
                some = gin.at[pl.ds(0, c)]
                remote(some, some, sent_sem.at[0], gin_recv.at[0], me, layer).wait_recv()

    def wait_parts(count, most, rows, copy_of):
        for c in range(1, most + 1):

            @pl.when(count == c)
            def _():
                copy_of(landing.at[pl.ds(0, c), rows])

    def wait_heard(rows, n):
        wait_parts(
            heard_count, pin.shape[0], rows,
            lambda some: remote(
                some, some, sent_sem.at[0], part_recv.at[n], me, layer
            ).wait_recv(),
        )

    def wait_shared(rows, n):
        wait_parts(
            shared_count, len(shared), rows,
            lambda some: remote(
                some, some, sent_sem.at[0], share_recv.at[n], me, layer
            ).wait_recv(),
        )

    def wait_sent():
        wait_parts(
            sent_count, landing.shape[0], pl.ds(0, packed),
            lambda some: remote(
                some, some, sent_sem.at[0], part_recv.at[0], me, layer
            ).wait_send(),
        )

    def wait_chunks():
        some = cin.at[pl.ds(1, ne - 1)]
        return remote(some, some, chunk_send.at[0], chunk_recv.at[0], me, layer)

    @pl.when(has_below)
    def _():
        halo_copy(1).start()

    @pl.when(has_above & jnp.logical_not(told))
    def _():
        halo_copy(0).start()

    @pl.when(has_above & odd & relayed)
    def _():
        greet(side_sem, me - 1, layer)

    for d in range(1, ne):

        @pl.when(me >= d)
        def _():
            greet(near_sem if d <= reach else far_sem, me - d, layer)

    row = lax.broadcasted_iota(jnp.int32, (atoms, atoms), 0)

    def one_hot(k, start):
        return jnp.where(row == near_ref[k : k + 1, :] - start, 1.0, 0.0).astype(BF16)

    def taken(blocks, hot):
        found = jnp.dot(blocks, hot, preferred_element_type=F32)
        return [found[:, t * LANES : (t + 1) * LANES] for t in range(tiles)]

    def pick_side(side):
        for t, found in enumerate(taken(halo[side], hots[side])):
            for n in range(2):
                gs[side, pl.ds(n * tiles + t, packed, stride=fold), :] = found

    load_near.wait()
    load_weight = load(1, weight_hbm, weight_ref)
    for j, k in enumerate(slots):
        for t, found in enumerate(taken(own[...], one_hot(k, atoms))):
            g3[pl.ds(t * size + j, packed, stride=pad), :] = found
    hots[0] = one_hot(0, 0)
    hots[1] = one_hot(1, 2 * atoms)

    @pl.when(told & has_above)
    def _():
        pl.semaphore_wait(side_sem, 1)
        halo_copy(0).start()

    @pl.when(near_above > 0)
    def _():
        pl.semaphore_wait(near_sem, near_above)

    for d in range(1, reach + 1):

        @pl.when(me + d < ne)
        def _():
            green_copy(d).start()

    both = has_above & has_below
    lower_first = lax.rem(layer, 2) == 1
    early = jnp.where(both, jnp.where(lower_first, 0, 1), jnp.where(has_above, 0, 1))
    late = 1 - early

    @pl.when(jnp.logical_not(both))
    def _():
        ps[early] = jnp.zeros(ps.shape[1:], F32)

    for d in range(1, reach + 1):

        @pl.when(me < d)
        def _():
            gin[d - 1] = jnp.zeros((packed, atoms), BF16)

    for slot in range(1, pin.shape[0]):

        @pl.when(jnp.logical_not(heard(slot)))
        def _():
            pin[slot] = jnp.zeros(pin.shape[1:], BF16)

    e16_ref[...] = expansion(order, depth, packed)
    load_coup.wait()
    load_shift = load(0, shift_hbm, shift_ref)
    for t in range(tiles):
        block = coup_ref[:, :, t * LANES : (t + 1) * LANES].astype(F32)
        block = block.reshape(order, order, nbr, LANES)
        c4[:, :, t * size : (t + 1) * size, :] = block[:, :, slots[0] :, :]
        for side in range(2):
            for n in range(2):
                at = n * tiles + t
                cx[side, :, :, at : at + 1, :] = block[:, :, side : side + 1, :]
    lower = lax.broadcasted_iota(jnp.int32, (order, fold, LANES), 1) < tiles
    for side in range(2):
        for i in range(0, order, 2):
            cp[side, i // 2] = jnp.where(lower, cx[side, i], cx[side, i + 1])

    last = off[-1] + 1
    pscr[last * pad :, :] = jnp.zeros(((packed - last) * pad, LANES), F32)
    for side in range(2):
        ps[side, last * fold :, :] = jnp.zeros(((packed - last) * fold, LANES), F32)

    def entries(p, rows):
        at = [off[min(p, q)] + abs(p - q) for q in range(order)]
        return [slice(a * rows, (a + 1) * rows) for a in at]

    def products():
        for i in range(0, order, 2):
            first = jnp.zeros((2, order, pad, LANES), F32)
            for p in range(order):
                block = jnp.stack([g3[at, :] for at in entries(p, pad)])
                first = first + c4[i : i + 2, p][:, None] * block[None]
            total = first[:, 0][:, None] * c4[i:, 0][None]
            for q in range(1, order):
                total = total + first[:, q][:, None] * c4[i:, q][None]
            total = total.astype(BF16).astype(F32)
            for n in range(2):
                pscr[off[i + n] * pad : (off[i + n] + order - i - n) * pad, :] = total[
                    n, n:
                ].reshape(-1, LANES)

    def side_products(side, start, stop):
        for i in range(start, stop, 2):
            first = jnp.zeros((order, fold, LANES), F32)
            for p in range(order):
                block = jnp.stack([gs[side, at, :] for at in entries(p, fold)])
                first = first + cp[side, i // 2, p][None] * block
            total = first[0][None] * cx[side, i:, 0]
            for q in range(1, order):
                total = total + first[q][None] * cx[side, i:, q]
            total = total.astype(BF16).astype(F32).reshape(-1, LANES)
            ps[side, off[i] * fold : off[i + 1] * fold, :] = total
            second = total[fold:].reshape(-1, fold, LANES)
            second = jnp.concatenate([second[:, tiles:], second[:, :tiles]], axis=1)
            ps[side, off[i + 1] * fold : (off[i + 1] + order - i - 1) * fold, :] = second.reshape(
                -1, LANES
            )

    products()

    load_weight.wait()
    load_shift.wait()

    def add_weights(w, sums):
        shift = shift_ref[w]
        low, high = weight_ref[w], weight_ref[freqs + w]
        new = []
        for d in range(1, reach + 1):
            pick = jnp.where(shift == d, 1.0, 0.0).astype(F32)
            new += [sums[2 * d - 2] + pick * low, sums[2 * d - 1] + pick * high]
        return tuple(new)

    sums = lax.fori_loop(
        0, freqs, add_weights, tuple(jnp.zeros((nbr, atoms), F32) for _ in range(2 * reach)),
        unroll=4,
    )
    for s in range(2 * reach):
        ab[s] = sums[s]
        for side in range(2):
            aw[side, s] = jnp.broadcast_to(sums[s][side : side + 1], aw.shape[2:])

    def rows_of(j, t, start, stop):
        at = start * pad + t * size + j
        return pscr[pl.ds(at, stop - start, stride=pad), :]

    def side_rows(side, t, start, stop):
        return ps[side, pl.ds(start * fold + t, stop - start, stride=fold), :]

    def side_partials(side, t, s, start, stop):
        lanes = slice(t * LANES, (t + 1) * LANES)
        weight = aw[side, s, 0:1, lanes]
        return pacc[s, start:stop, lanes] + weight * side_rows(side, t, start, stop)

    for t in range(tiles):
        lanes = slice(t * LANES, (t + 1) * LANES)
        for s in range(2 * reach):
            total = None
            for j, k in enumerate(slots):
                term = ab[s, k : k + 1, lanes] * rows_of(j, t, 0, packed)
                total = term if total is None else total + term
            pacc[s, :, lanes] = total

    g16[...] = jnp.zeros_like(g16)
    for p in range(order):
        g16[p, :order, :] = green_ref[p].astype(F32)
    sig_ref[...] = jnp.zeros_like(sig_ref)

    @pl.when(both & lower_first)
    def _():
        halo_copy(0).wait_recv()

    @pl.when(both & jnp.logical_not(lower_first))
    def _():
        halo_copy(1).wait_recv()

    @pl.when(both)
    def _():
        pick_side(early)
        side_products(early, 0, order)
        for t in range(tiles):
            for s in range(2 * reach):
                pacc[s, :, t * LANES : (t + 1) * LANES] = side_partials(early, t, s, 0, packed)

    @pl.when(late == 0)
    def _():
        halo_copy(0).wait_recv()

    @pl.when(late == 1)
    def _():
        halo_copy(1).wait_recv()

    pick_side(late)

    def correlations():
        @pl.when(far_above > 0)
        def _():
            pl.semaphore_wait(far_sem, far_above)

        wait_gin()

        index = lax.broadcasted_iota(jnp.int32, (packed, LANES), 0)
        twice = jnp.full((packed, LANES), 2.0, F32)
        for p in range(order):
            twice = jnp.where(index == off[p], 1.0, twice)
        rows = [[None] * tiles for _ in range(reach * nbr)]

        for t in range(tiles):
            greens = [
                gin[d, :, t * LANES : (t + 1) * LANES].astype(F32) * twice for d in range(reach)
            ]
            for k in range(nbr):
                if k < 2:
                    value = side_rows(k, t, 0, packed)
                else:
                    value = rows_of(k - 2, t, 0, packed)
                for d in range(reach):
                    rows[d * nbr + k][t] = jnp.sum(greens[d] * value, axis=0, keepdims=True)

        sums = [jnp.concatenate([r[t] for r in rows], axis=0) for t in range(tiles)]
        lane = lax.broadcasted_iota(jnp.int32, sums[0].shape, 1)
        for e in range(ne):
            start = e * share % LANES
            low, high = e * share // LANES, (e * share + share - 1) // LANES
            chunks[e] = sums[low] if low == high else jnp.where(lane >= start, sums[low], sums[high])
        for r in range(1, ne):
            chunk_copy(r).start()

    for n, (start, stop, first, final) in enumerate(plan):
        if first < final:
            side_products(late, first, final)
            if final == order:
                pl.when(me >= ne // 2)(correlations)
        for t in range(tiles):
            lanes = slice(t * LANES, (t + 1) * LANES)
            for s in range(2 * reach):
                pout[s, start:stop, lanes] = side_partials(late, t, s, start, stop).astype(BF16)

        @pl.when(even)
        def _():
            for e, slot in straight[0]:

                @pl.when(reaches(me + e))
                def _():
                    part_copy(outgoing(e), pin.at[slot], start, stop, e).start()

            for number, (e, _) in enumerate(shared):

                @pl.when(reaches(me + e))
                def _():
                    share_copy(outgoing(e), number, start, stop).start()

            part_copy(outgoing(1), pin.at[0], start, stop, 1).start()

        @pl.when(odd)
        def _():
            for e, slot in straight[1]:

                @pl.when(reaches(me + e))
                def _():
                    part_copy(outgoing(e), pin.at[slot], start, stop, e).start()

            part_copy(outgoing(-1), pin.at[0], start, stop, -1).start()

    pl.when(me < ne // 2)(correlations)

    @pl.when(odd)
    def _():
        for n, (start, stop) in enumerate(arrivals):
            wait_shared(pl.ds(start, stop - start), n)
            for number, (e, slot) in enumerate(shared):
                out = outgoing(e - 1)

                @pl.when(reaches(base + e))
                def _():
                    for t in range(tiles):
                        lanes = slice(t * LANES, (t + 1) * LANES)
                        total = side_partials(late, t, out, start, stop)
                        total = total + given[number, start:stop, lanes].astype(F32)
                        pout[out, start:stop, lanes] = total.astype(BF16)
                    part_copy(out, pin.at[slot], start, stop, e - 1).start()

    for n, (start, stop) in enumerate(arrivals):
        first, final = complete(order, start), complete(order, stop)
        wait_heard(pl.ds(start, stop - start), n)
        sigma = pin[0, start:stop].astype(F32)
        for s in range(1, pin.shape[0]):
            sigma = sigma + pin[s, start:stop].astype(F32)
        sig_ref[start:stop, :] = sigma.astype(BF16)
        s16[first:final] = jnp.dot(
            e16_ref[first * depth : final * depth, :], sig_ref[...], preferred_element_type=F32
        ).reshape(final - first, depth, atoms)
        for i in range(0, order, 2):
            left = [None if first == 0 else l16[i + m] for m in range(2)]
            for p in range(first, final):
                block = s16[p]
                for m in range(2):
                    term = g16[i + m, p : p + 1, :] * block
                    left[m] = term if left[m] is None else left[m] + term
            for m in range(2):
                l16[i + m] = left[m].astype(BF16).astype(F32) if stop == packed else left[m]

    for i in range(0, order, 2):
        total = [g16[i + n] for n in range(2)]
        for p in range(order):
            block = g16[p]
            total = [total[n] + l16[i + n, p : p + 1, :] * block for n in range(2)]
        for n in range(2):
            cor_ref[i + n] = total[n][:order].astype(BF16)

    wait_chunks().wait_recv()
    summed = chunks[me]
    for r in range(1, ne):
        summed = summed + cin[r]
    summed = pltpu.roll(summed, lax.rem(ne * LANES - me * share, LANES), 1)
    summed = summed[:, :share] * (1.0 / (order * math.sqrt(ne)))
    for w in range(freqs):
        shift = shift_ref[w]
        value = summed[(reach - 1) * nbr :]
        for d in range(1, reach):
            value = jnp.where(shift == d, summed[(d - 1) * nbr : d * nbr], value)
        pol_ref[w] = value

    wait_sent()
    wait_chunks().wait_send()


def finish(cor_ref, pol_ref, cor_hbm, pol_hbm, sem):
    first = pltpu.make_async_copy(cor_ref, cor_hbm, sem.at[0])
    second = pltpu.make_async_copy(pol_ref, pol_hbm, sem.at[1])
    first.start()
    second.start()
    first.wait()
    second.wait()


def body(green_blocks, coupling, phonon_weights, neighbours, phonon_shifts):
    ne = lax.axis_size("energy")
    reach = max(ne // 4, 1)
    order = green_blocks.shape[1]
    atoms = green_blocks.shape[3]
    nbr = neighbours.shape[0]
    freqs = phonon_shifts.shape[0]
    tiles = atoms // LANES
    share = atoms // ne
    count = order * (order + 1) // 2
    packed = -(-count // 16) * 16
    pad = -(-(tiles * (nbr - 2)) // 8) * 8
    fold = -(-(2 * tiles) // 8) * 8
    rows = 16 * (-(-order // 16))
    parts = len(segments(order, packed)) - 1
    vmem = pl.BlockSpec(memory_space=pltpu.VMEM)
    hbm = pl.BlockSpec(memory_space=pltpu.HBM)
    dma = pltpu.SemaphoreType.DMA
    green = green_blocks[0]
    staged = pl.pallas_call(
        functools.partial(kernel, reach),
        out_shape=(
            jax.ShapeDtypeStruct((order, order, atoms), BF16),
            jax.ShapeDtypeStruct((freqs, nbr, share), F32),
        ),
        in_specs=[hbm] * 5,
        out_specs=(vmem, vmem),
        scratch_shapes=[
            pltpu.SMEM((freqs,), jnp.int32),
            pltpu.VMEM((order, order, atoms), BF16),
            pltpu.VMEM((order * order, nbr, atoms), BF16),
            pltpu.VMEM((2 * freqs, nbr, atoms), F32),
            pltpu.VMEM((nbr, atoms), jnp.int32),
            pltpu.VMEM((order * rows, packed), BF16),
            pltpu.VMEM((packed, atoms), BF16),
            pltpu.VMEM((order, rows, atoms), F32),
            pltpu.VMEM((order, rows, atoms), F32),
            pltpu.VMEM((order, rows, atoms), F32),
            pltpu.VMEM((packed, atoms), F32),
            pltpu.VMEM((packed, atoms), BF16),
            pltpu.VMEM((2, packed, atoms), BF16),
            pltpu.VMEM((reach, packed, atoms), BF16),
            pltpu.VMEM((2 * reach, packed, atoms), BF16),
            pltpu.VMEM((1 + 2 * ((reach + 1) // 2), packed, atoms), BF16),
            pltpu.VMEM((max(len(routes(reach)[1]), 1), packed, atoms), BF16),
            pltpu.VMEM((4 + 3 * reach, packed, atoms), BF16),
            pltpu.VMEM((2 * reach, packed, atoms), F32),
            pltpu.VMEM((2, atoms, atoms), BF16),
            pltpu.VMEM((ne, reach * nbr, LANES), F32),
            pltpu.VMEM((ne, reach * nbr, LANES), F32),
            pltpu.VMEM((order, order, pad, LANES), F32),
            pltpu.VMEM((packed * pad, LANES), F32),
            pltpu.VMEM((packed * pad, LANES), F32),
            pltpu.VMEM((2, order, order, fold, LANES), F32),
            pltpu.VMEM((2, order // 2, order, fold, LANES), F32),
            pltpu.VMEM((2, packed * fold, LANES), F32),
            pltpu.VMEM((2, packed * fold, LANES), F32),
            pltpu.VMEM((2 * reach, nbr, atoms), F32),
            pltpu.VMEM((2, 2 * reach, 8, atoms), F32),
            dma((2,)), *[pltpu.SemaphoreType.REGULAR] * 3,
            dma((1,)), dma((2,)), dma((1,)), dma((parts,)), dma((parts,)), dma((1,)), dma((1,)),
        ],
        compiler_params=pltpu.CompilerParams(
            collective_id=0, has_side_effects=True, vmem_limit_bytes=VMEM_LIMIT
        ),
    )(
        *(
            pltpu.with_memory_space_constraint(x, pltpu.HBM)
            for x in (
                phonon_shifts,
                green,
                coupling.reshape(order * order, nbr, atoms),
                phonon_weights.reshape(2 * freqs, nbr, atoms),
                neighbours,
            )
        )
    )
    corrected, polarization = pl.pallas_call(
        finish,
        out_shape=(
            jax.ShapeDtypeStruct((order, order, atoms), BF16),
            jax.ShapeDtypeStruct((freqs, nbr, share), F32),
        ),
        in_specs=[vmem, vmem],
        out_specs=(hbm, hbm),
        scratch_shapes=[dma((2,))],
        compiler_params=pltpu.CompilerParams(vmem_limit_bytes=VMEM_LIMIT),
    )(*staged)
    return corrected[None], polarization


def solution(mesh):
    return jax.shard_map(
        body,
        mesh=mesh,
        in_specs=(
            P("energy", None, None, "layer"),
            P(None, None, None, "layer"),
            P(None, None, None, "layer"),
            P(None, "layer"),
            P(),
        ),
        out_specs=(P("energy", None, None, "layer"), P(None, None, ("layer", "energy"))),
        check_vma=False,
    )
```

```python
import functools
import math

import jax
import jax.numpy as jnp
from jax import lax
from jax.experimental import pallas as pl
from jax.experimental.pallas import tpu as pltpu
from jax.sharding import PartitionSpec as P

MESH = pl.DeviceIdType.MESH
LANES = 128
F32 = jnp.float32
BF16 = jnp.bfloat16
VMEM_LIMIT = 48 * 1024 * 1024


def offsets(order):
    return [p * order - p * (p - 1) // 2 for p in range(order)]


def segments(order, packed):
    stops = [16] + [o // 16 * 16 for o in offsets(order)[8::4]] + [packed]
    plan, start, first = [], 0, 0
    for stop in stops:
        if stop > start:
            final = 2 if start == 0 else order
            plan.append((start, stop, first, final))
            start, first = stop, final
    return plan


def routes(reach):
    straight, shared = ([], []), []
    for d in range(1, (reach + 1) // 2 + 1):
        for way in (1, -1):
            slot = 2 * d - (way > 0)
            for parity in range(2):
                far = [abs(2 * d * way + parity - p) for p in range(2)]
                near = [p for p in range(2) if far[p] <= reach]
                if len(near) == 2:
                    shared.append((2 * d * way + parity, slot))
                elif near:
                    straight[near[0]].append((2 * d * way + parity - near[0], slot))
    return straight, shared


def complete(order, stop):
    return sum(o + order - p <= stop for p, o in enumerate(offsets(order)))


def expansion(order, row_stride, packed_rows):
    row = lax.broadcasted_iota(jnp.int32, (order * row_stride, packed_rows), 0)
    column = lax.broadcasted_iota(jnp.int32, (order * row_stride, packed_rows), 1)
    p, q = row // row_stride, row % row_stride
    low, high = jnp.minimum(p, q), jnp.maximum(p, q)
    entry = low * order - low * (low - 1) // 2 + high - low
    return jnp.where((entry == column) & (q < order), 1.0, 0.0).astype(BF16)


def kernel(
    reach, shift_hbm, green_hbm, coup_hbm, weight_hbm, near_hbm, cor_ref, pol_ref,
    shift_ref, green_ref, coup_ref, weight_ref, near_ref, e16_ref, sig_ref,
    g16, s16, l16, tri32, own, halo, gin, pout, pin, given, landing, pacc, hots, chunks, cin, c4, g3, pscr, cx, cp, gs, ps, ab, aw,
    load_sem, side_sem, near_sem, far_sem, sent_sem, halo_recv, gin_recv, part_recv, share_recv,
    chunk_send, chunk_recv,
):
    order = green_ref.shape[0]
    atoms = green_ref.shape[2]
    nbr = near_ref.shape[0]
    freqs = shift_ref.shape[0]
    tiles = atoms // LANES
    packed = own.shape[0]
    pad = c4.shape[2]
    fold = cx.shape[3]
    ne = lax.axis_size("energy")
    nl = lax.axis_size("layer")
    me = lax.axis_index("energy")
    layer = lax.axis_index("layer")
    share = atoms // ne
    depth = s16.shape[1]
    off = offsets(order)
    plan = segments(order, packed)
    slots = tuple(range(2, nbr))
    size = len(slots)

    def load(n, src, dst):
        copy = pltpu.make_async_copy(src, dst, load_sem.at[n])
        copy.start()
        return copy

    step = order // 4
    for p in range(0, order, step):
        load(0, green_hbm.at[pl.ds(p, step)], green_ref.at[pl.ds(p, step)])
    load_green = pltpu.make_async_copy(green_hbm, green_ref, load_sem.at[0])
    load_near = load(1, near_hbm, near_ref)

    barrier = pltpu.get_barrier_semaphore()

    def greet(sem, energy, row):
        pl.semaphore_signal(
            sem, inc=1, device_id={"energy": energy, "layer": row}, device_id_type=MESH
        )

    odd = lax.rem(me, 2) == 1
    even = jnp.logical_not(odd)
    relayed = me >= ne - 2
    told = even & relayed
    has_above, has_below = layer < nl - 1, layer > 0
    near_above = jnp.minimum(ne - 1 - me, reach)
    near_count = near_above + jnp.minimum(me, reach)
    far_above = ne - 1 - me - near_above

    @pl.when(has_below)
    def _():
        greet(barrier, me + told.astype(jnp.int32), layer - 1)

    @pl.when(odd)
    def _():
        greet(barrier, me - 1, layer)

    @pl.when(has_above)
    def _():
        greet(barrier, me, layer + 1)

    for d in range(1, ne):

        @pl.when(me + d < ne)
        def _():
            greet(barrier, me + d, layer)

    tri32[...] = jnp.zeros_like(tri32)
    load_green.wait()
    load_coup = load(0, coup_hbm, coup_ref)
    for p in range(order):
        tri32[off[p] : off[p] + order - p, :] = green_ref[p].astype(F32)[p:, :]
    own[...] = tri32[...].astype(BF16)

    pl.semaphore_wait(
        barrier,
        me
        + even.astype(jnp.int32)
        + has_below.astype(jnp.int32)
        + jnp.where(told, 0, jnp.where(relayed, 2, 1)) * has_above.astype(jnp.int32),
    )

    def remote(src, dst, send, recv, energy, row):
        return pltpu.make_async_remote_copy(
            src_ref=src, dst_ref=dst, send_sem=send, recv_sem=recv,
            device_id={"energy": energy, "layer": row}, device_id_type=MESH,
        )

    straight, shared = routes(reach)
    base = me - lax.rem(me, 2)

    def reaches(offset):
        return (offset >= 0) & (offset < ne)

    def heard(slot):
        d = (slot + 1) // 2
        if slot % 2:
            return (base >= 2 * d) & (2 * d - even.astype(jnp.int32) <= reach)
        return (base + 2 * d < ne) & (2 * d - odd.astype(jnp.int32) <= reach)

    def number(conditions):
        total = 0
        for condition in conditions:
            total = total + condition.astype(jnp.int32)
        return total

    heard_count = 1 + number([heard(slot) for slot in range(1, pin.shape[0])])
    shared_count = number([reaches(base + e) for e, _ in shared])
    sent_count = 1 + shared_count + near_above + number([has_above, has_below])
    for parity in range(2):
        which = odd if parity else even
        sent_count = sent_count + number([which & reaches(me + e) for e, _ in straight[parity]])

    def halo_copy(side):
        row = layer + 1 if side == 0 else layer - 1
        return remote(own, halo.at[side], sent_sem.at[0], halo_recv.at[side], me, row)

    def green_copy(d):
        return remote(
            own, gin.at[d - 1], sent_sem.at[0], gin_recv.at[0], me + d, layer
        )

    arrivals = [(0, plan[1][1])] + [(start, stop) for start, stop, _, _ in plan[2:]]

    def group(start):
        return sum(start >= stop for _, stop in arrivals)

    def part_copy(source, target, start, stop, e):
        rows = pl.ds(start, stop - start)
        return remote(
            pout.at[source, rows], target.at[rows], sent_sem.at[0],
            part_recv.at[group(start)], me + e, layer,
        )

    def share_copy(source, number, start, stop):
        rows = pl.ds(start, stop - start)
        return remote(
            pout.at[source, rows], given.at[number, rows], sent_sem.at[0], share_recv.at[group(start)],
            me + 1, layer,
        )

    def outgoing(offset):
        return 2 * offset - 2 if offset > 0 else -2 * offset - 1

    def chunk_copy(r):
        dest = lax.rem(me + r, ne)
        return remote(
            chunks.at[dest], cin.at[r], chunk_send.at[0], chunk_recv.at[0], dest, layer
        )

    def wait_gin():
        for c in range(1, reach + 1):

            @pl.when(jnp.minimum(me, reach) == c)
            def _():
                some = gin.at[pl.ds(0, c)]
                remote(some, some, sent_sem.at[0], gin_recv.at[0], me, layer).wait_recv()

    def wait_parts(count, most, rows, copy_of):
        for c in range(1, most + 1):

            @pl.when(count == c)
            def _():
                copy_of(landing.at[pl.ds(0, c), rows])

    def wait_heard(rows, n):
        wait_parts(
            heard_count, pin.shape[0], rows,
            lambda some: remote(
                some, some, sent_sem.at[0], part_recv.at[n], me, layer
            ).wait_recv(),
        )

    def wait_shared(rows, n):
        wait_parts(
            shared_count, len(shared), rows,
            lambda some: remote(
                some, some, sent_sem.at[0], share_recv.at[n], me, layer
            ).wait_recv(),
        )

    def wait_sent():
        wait_parts(
            sent_count, landing.shape[0], pl.ds(0, packed),
            lambda some: remote(
                some, some, sent_sem.at[0], part_recv.at[0], me, layer
            ).wait_send(),
        )

    def wait_chunks():
        some = cin.at[pl.ds(1, ne - 1)]
        return remote(some, some, chunk_send.at[0], chunk_recv.at[0], me, layer)

    @pl.when(has_below)
    def _():
        halo_copy(1).start()

    @pl.when(has_above & jnp.logical_not(told))
    def _():
        halo_copy(0).start()

    @pl.when(has_above & odd & relayed)
    def _():
        greet(side_sem, me - 1, layer)

    for d in range(1, ne):

        @pl.when(me >= d)
        def _():
            greet(near_sem if d <= reach else far_sem, me - d, layer)

    row = lax.broadcasted_iota(jnp.int32, (atoms, atoms), 0)

    def one_hot(k, start):
        return jnp.where(row == near_ref[k : k + 1, :] - start, 1.0, 0.0).astype(BF16)

    def taken(blocks, hot):
        found = jnp.dot(blocks, hot, preferred_element_type=F32)
        return [found[:, t * LANES : (t + 1) * LANES] for t in range(tiles)]

    def pick_side(side):
        for t, found in enumerate(taken(halo[side], hots[side])):
            for n in range(2):
                gs[side, pl.ds(n * tiles + t, packed, stride=fold), :] = found

    load_near.wait()
    load_weight = load(1, weight_hbm, weight_ref)
    for j, k in enumerate(slots):
        for t, found in enumerate(taken(own[...], one_hot(k, atoms))):
            g3[pl.ds(t * size + j, packed, stride=pad), :] = found
    hots[0] = one_hot(0, 0)
    hots[1] = one_hot(1, 2 * atoms)

    @pl.when(told & has_above)
    def _():
        pl.semaphore_wait(side_sem, 1)
        halo_copy(0).start()

    @pl.when(near_above > 0)
    def _():
        pl.semaphore_wait(near_sem, near_above)

    for d in range(1, reach + 1):

        @pl.when(me + d < ne)
        def _():
            green_copy(d).start()

    both = has_above & has_below
    lower_first = lax.rem(layer, 2) == 1
    early = jnp.where(both, jnp.where(lower_first, 0, 1), jnp.where(has_above, 0, 1))
    late = 1 - early

    @pl.when(jnp.logical_not(both))
    def _():
        ps[early] = jnp.zeros(ps.shape[1:], F32)

    for d in range(1, reach + 1):

        @pl.when(me < d)
        def _():
            gin[d - 1] = jnp.zeros((packed, atoms), BF16)

    for slot in range(1, pin.shape[0]):

        @pl.when(jnp.logical_not(heard(slot)))
        def _():
            pin[slot] = jnp.zeros(pin.shape[1:], BF16)

    e16_ref[...] = expansion(order, depth, packed)
    load_coup.wait()
    load_shift = load(0, shift_hbm, shift_ref)
    for t in range(tiles):
        block = coup_ref[:, :, t * LANES : (t + 1) * LANES].astype(F32)
        block = block.reshape(order, order, nbr, LANES)
        c4[:, :, t * size : (t + 1) * size, :] = block[:, :, slots[0] :, :]
        for side in range(2):
            for n in range(2):
                at = n * tiles + t
                cx[side, :, :, at : at + 1, :] = block[:, :, side : side + 1, :]
    lower = lax.broadcasted_iota(jnp.int32, (order, fold, LANES), 1) < tiles
    for side in range(2):
        for i in range(0, order, 2):
            cp[side, i // 2] = jnp.where(lower, cx[side, i], cx[side, i + 1])

    last = off[-1] + 1
    pscr[last * pad :, :] = jnp.zeros(((packed - last) * pad, LANES), F32)
    for side in range(2):
        ps[side, last * fold :, :] = jnp.zeros(((packed - last) * fold, LANES), F32)

    def entries(p, rows):
        at = [off[min(p, q)] + abs(p - q) for q in range(order)]
        return [slice(a * rows, (a + 1) * rows) for a in at]

    def products():
        for i in range(0, order, 2):
            first = jnp.zeros((2, order, pad, LANES), F32)
            for p in range(order):
                block = jnp.stack([g3[at, :] for at in entries(p, pad)])
                first = first + c4[i : i + 2, p][:, None] * block[None]
            total = first[:, 0][:, None] * c4[i:, 0][None]
            for q in range(1, order):
                total = total + first[:, q][:, None] * c4[i:, q][None]
            total = total.astype(BF16).astype(F32)
            for n in range(2):
                pscr[off[i + n] * pad : (off[i + n] + order - i - n) * pad, :] = total[
                    n, n:
                ].reshape(-1, LANES)

    def side_products(side, start, stop):
        for i in range(start, stop, 2):
            first = jnp.zeros((order, fold, LANES), F32)
            for p in range(order):
                block = jnp.stack([gs[side, at, :] for at in entries(p, fold)])
                first = first + cp[side, i // 2, p][None] * block
            total = first[0][None] * cx[side, i:, 0]
            for q in range(1, order):
                total = total + first[q][None] * cx[side, i:, q]
            total = total.astype(BF16).astype(F32).reshape(-1, LANES)
            ps[side, off[i] * fold : off[i + 1] * fold, :] = total
            second = total[fold:].reshape(-1, fold, LANES)
            second = jnp.concatenate([second[:, tiles:], second[:, :tiles]], axis=1)
            ps[side, off[i + 1] * fold : (off[i + 1] + order - i - 1) * fold, :] = second.reshape(
                -1, LANES
            )

    products()

    load_weight.wait()
    load_shift.wait()

    def add_weights(w, sums):
        shift = shift_ref[w]
        low, high = weight_ref[w], weight_ref[freqs + w]
        new = []
        for d in range(1, reach + 1):
            pick = jnp.where(shift == d, 1.0, 0.0).astype(F32)
            new += [sums[2 * d - 2] + pick * low, sums[2 * d - 1] + pick * high]
        return tuple(new)

    sums = lax.fori_loop(
        0, freqs, add_weights, tuple(jnp.zeros((nbr, atoms), F32) for _ in range(2 * reach)),
        unroll=4,
    )
    for s in range(2 * reach):
        ab[s] = sums[s]
        for side in range(2):
            aw[side, s] = jnp.broadcast_to(sums[s][side : side + 1], aw.shape[2:])

    def rows_of(j, t, start, stop):
        at = start * pad + t * size + j
        return pscr[pl.ds(at, stop - start, stride=pad), :]

    def side_rows(side, t, start, stop):
        return ps[side, pl.ds(start * fold + t, stop - start, stride=fold), :]

    def side_partials(side, t, s, start, stop):
        lanes = slice(t * LANES, (t + 1) * LANES)
        weight = aw[side, s, 0:1, lanes]
        return pacc[s, start:stop, lanes] + weight * side_rows(side, t, start, stop)

    for t in range(tiles):
        lanes = slice(t * LANES, (t + 1) * LANES)
        for s in range(2 * reach):
            total = None
            for j, k in enumerate(slots):
                term = ab[s, k : k + 1, lanes] * rows_of(j, t, 0, packed)
                total = term if total is None else total + term
            pacc[s, :, lanes] = total

    g16[...] = jnp.zeros_like(g16)
    for p in range(order):
        g16[p, :order, :] = green_ref[p].astype(F32)
    sig_ref[...] = jnp.zeros_like(sig_ref)

    @pl.when(both & lower_first)
    def _():
        halo_copy(0).wait_recv()

    @pl.when(both & jnp.logical_not(lower_first))
    def _():
        halo_copy(1).wait_recv()

    @pl.when(both)
    def _():
        pick_side(early)
        side_products(early, 0, order)
        for t in range(tiles):
            for s in range(2 * reach):
                pacc[s, :, t * LANES : (t + 1) * LANES] = side_partials(early, t, s, 0, packed)

    @pl.when(late == 0)
    def _():
        halo_copy(0).wait_recv()

    @pl.when(late == 1)
    def _():
        halo_copy(1).wait_recv()

    pick_side(late)

    def correlations():
        @pl.when(far_above > 0)
        def _():
            pl.semaphore_wait(far_sem, far_above)

        wait_gin()

        index = lax.broadcasted_iota(jnp.int32, (packed, LANES), 0)
        twice = jnp.full((packed, LANES), 2.0, F32)
        for p in range(order):
            twice = jnp.where(index == off[p], 1.0, twice)
        rows = [[None] * tiles for _ in range(reach * nbr)]

        for t in range(tiles):
            greens = [
                gin[d, :, t * LANES : (t + 1) * LANES].astype(F32) * twice for d in range(reach)
            ]
            for k in range(nbr):
                if k < 2:
                    value = side_rows(k, t, 0, packed)
                else:
                    value = rows_of(k - 2, t, 0, packed)
                for d in range(reach):
                    rows[d * nbr + k][t] = jnp.sum(greens[d] * value, axis=0, keepdims=True)

        sums = [jnp.concatenate([r[t] for r in rows], axis=0) for t in range(tiles)]
        lane = lax.broadcasted_iota(jnp.int32, sums[0].shape, 1)
        for e in range(ne):
            start = e * share % LANES
            low, high = e * share // LANES, (e * share + share - 1) // LANES
            chunks[e] = sums[low] if low == high else jnp.where(lane >= start, sums[low], sums[high])
        for r in range(1, ne):
            chunk_copy(r).start()

    def hand_out(n):
        start, stop, _, _ = plan[n]
        for t in range(tiles):
            lanes = slice(t * LANES, (t + 1) * LANES)
            for s in range(2 * reach):
                pout[s, start:stop, lanes] = side_partials(late, t, s, start, stop).astype(BF16)

        @pl.when(even)
        def _():
            for e, slot in straight[0]:

                @pl.when(reaches(me + e))
                def _():
                    part_copy(outgoing(e), pin.at[slot], start, stop, e).start()

            for number, (e, _) in enumerate(shared):

                @pl.when(reaches(me + e))
                def _():
                    share_copy(outgoing(e), number, start, stop).start()

            part_copy(outgoing(1), pin.at[0], start, stop, 1).start()

        @pl.when(odd)
        def _():
            for e, slot in straight[1]:

                @pl.when(reaches(me + e))
                def _():
                    part_copy(outgoing(e), pin.at[slot], start, stop, e).start()

            part_copy(outgoing(-1), pin.at[0], start, stop, -1).start()

    for n, (start, stop, first, final) in enumerate(plan):
        if first < final:
            side_products(late, first, final)
            if final == order:
                pl.when(me >= ne // 2)(correlations)
        if final < order and n == 0:
            pl.when(me < ne // 2)(functools.partial(hand_out, n))
        else:
            if n == 1:
                pl.when(me >= ne // 2)(functools.partial(hand_out, 0))
            hand_out(n)

    pl.when(me < ne // 2)(correlations)

    @pl.when(odd)
    def _():
        for n, (start, stop) in enumerate(arrivals):
            wait_shared(pl.ds(start, stop - start), n)
            for number, (e, slot) in enumerate(shared):
                out = outgoing(e - 1)

                @pl.when(reaches(base + e))
                def _():
                    for t in range(tiles):
                        lanes = slice(t * LANES, (t + 1) * LANES)
                        total = side_partials(late, t, out, start, stop)
                        total = total + given[number, start:stop, lanes].astype(F32)
                        pout[out, start:stop, lanes] = total.astype(BF16)
                    part_copy(out, pin.at[slot], start, stop, e - 1).start()

    for n, (start, stop) in enumerate(arrivals):
        first, final = complete(order, start), complete(order, stop)
        wait_heard(pl.ds(start, stop - start), n)
        sigma = pin[0, start:stop].astype(F32)
        for s in range(1, pin.shape[0]):
            sigma = sigma + pin[s, start:stop].astype(F32)
        sig_ref[start:stop, :] = sigma.astype(BF16)
        s16[first:final] = jnp.dot(
            e16_ref[first * depth : final * depth, :], sig_ref[...], preferred_element_type=F32
        ).reshape(final - first, depth, atoms)
        for i in range(0, order, 2):
            left = [None if first == 0 else l16[i + m] for m in range(2)]
            for p in range(first, final):
                block = s16[p]
                for m in range(2):
                    term = g16[i + m, p : p + 1, :] * block
                    left[m] = term if left[m] is None else left[m] + term
            for m in range(2):
                l16[i + m] = left[m].astype(BF16).astype(F32) if stop == packed else left[m]

    for i in range(0, order, 2):
        total = [g16[i + n] for n in range(2)]
        for p in range(order):
            block = g16[p]
            total = [total[n] + l16[i + n, p : p + 1, :] * block for n in range(2)]
        for n in range(2):
            cor_ref[i + n] = total[n][:order].astype(BF16)

    wait_chunks().wait_recv()
    summed = chunks[me]
    for r in range(1, ne):
        summed = summed + cin[r]
    summed = pltpu.roll(summed, lax.rem(ne * LANES - me * share, LANES), 1)
    summed = summed[:, :share] * (1.0 / (order * math.sqrt(ne)))
    for w in range(freqs):
        shift = shift_ref[w]
        value = summed[(reach - 1) * nbr :]
        for d in range(1, reach):
            value = jnp.where(shift == d, summed[(d - 1) * nbr : d * nbr], value)
        pol_ref[w] = value

    wait_sent()
    wait_chunks().wait_send()


def finish(cor_ref, pol_ref, cor_hbm, pol_hbm, sem):
    first = pltpu.make_async_copy(cor_ref, cor_hbm, sem.at[0])
    second = pltpu.make_async_copy(pol_ref, pol_hbm, sem.at[1])
    first.start()
    second.start()
    first.wait()
    second.wait()


def body(green_blocks, coupling, phonon_weights, neighbours, phonon_shifts):
    ne = lax.axis_size("energy")
    reach = max(ne // 4, 1)
    order = green_blocks.shape[1]
    atoms = green_blocks.shape[3]
    nbr = neighbours.shape[0]
    freqs = phonon_shifts.shape[0]
    tiles = atoms // LANES
    share = atoms // ne
    count = order * (order + 1) // 2
    packed = -(-count // 16) * 16
    pad = -(-(tiles * (nbr - 2)) // 8) * 8
    fold = -(-(2 * tiles) // 8) * 8
    rows = 16 * (-(-order // 16))
    parts = len(segments(order, packed)) - 1
    vmem = pl.BlockSpec(memory_space=pltpu.VMEM)
    hbm = pl.BlockSpec(memory_space=pltpu.HBM)
    dma = pltpu.SemaphoreType.DMA
    green = green_blocks[0]
    staged = pl.pallas_call(
        functools.partial(kernel, reach),
        out_shape=(
            jax.ShapeDtypeStruct((order, order, atoms), BF16),
            jax.ShapeDtypeStruct((freqs, nbr, share), F32),
        ),
        in_specs=[hbm] * 5,
        out_specs=(vmem, vmem),
        scratch_shapes=[
            pltpu.SMEM((freqs,), jnp.int32),
            pltpu.VMEM((order, order, atoms), BF16),
            pltpu.VMEM((order * order, nbr, atoms), BF16),
            pltpu.VMEM((2 * freqs, nbr, atoms), F32),
            pltpu.VMEM((nbr, atoms), jnp.int32),
            pltpu.VMEM((order * rows, packed), BF16),
            pltpu.VMEM((packed, atoms), BF16),
            pltpu.VMEM((order, rows, atoms), F32),
            pltpu.VMEM((order, rows, atoms), F32),
            pltpu.VMEM((order, rows, atoms), F32),
            pltpu.VMEM((packed, atoms), F32),
            pltpu.VMEM((packed, atoms), BF16),
            pltpu.VMEM((2, packed, atoms), BF16),
            pltpu.VMEM((reach, packed, atoms), BF16),
            pltpu.VMEM((2 * reach, packed, atoms), BF16),
            pltpu.VMEM((1 + 2 * ((reach + 1) // 2), packed, atoms), BF16),
            pltpu.VMEM((max(len(routes(reach)[1]), 1), packed, atoms), BF16),
            pltpu.VMEM((4 + 3 * reach, packed, atoms), BF16),
            pltpu.VMEM((2 * reach, packed, atoms), F32),
            pltpu.VMEM((2, atoms, atoms), BF16),
            pltpu.VMEM((ne, reach * nbr, LANES), F32),
            pltpu.VMEM((ne, reach * nbr, LANES), F32),
            pltpu.VMEM((order, order, pad, LANES), F32),
            pltpu.VMEM((packed * pad, LANES), F32),
            pltpu.VMEM((packed * pad, LANES), F32),
            pltpu.VMEM((2, order, order, fold, LANES), F32),
            pltpu.VMEM((2, order // 2, order, fold, LANES), F32),
            pltpu.VMEM((2, packed * fold, LANES), F32),
            pltpu.VMEM((2, packed * fold, LANES), F32),
            pltpu.VMEM((2 * reach, nbr, atoms), F32),
            pltpu.VMEM((2, 2 * reach, 8, atoms), F32),
            dma((2,)), *[pltpu.SemaphoreType.REGULAR] * 3,
            dma((1,)), dma((2,)), dma((1,)), dma((parts,)), dma((parts,)), dma((1,)), dma((1,)),
        ],
        compiler_params=pltpu.CompilerParams(
            collective_id=0, has_side_effects=True, vmem_limit_bytes=VMEM_LIMIT
        ),
    )(
        *(
            pltpu.with_memory_space_constraint(x, pltpu.HBM)
            for x in (
                phonon_shifts,
                green,
                coupling.reshape(order * order, nbr, atoms),
                phonon_weights.reshape(2 * freqs, nbr, atoms),
                neighbours,
            )
        )
    )
    corrected, polarization = pl.pallas_call(
        finish,
        out_shape=(
            jax.ShapeDtypeStruct((order, order, atoms), BF16),
            jax.ShapeDtypeStruct((freqs, nbr, share), F32),
        ),
        in_specs=[vmem, vmem],
        out_specs=(hbm, hbm),
        scratch_shapes=[dma((2,))],
        compiler_params=pltpu.CompilerParams(vmem_limit_bytes=VMEM_LIMIT),
    )(*staged)
    return corrected[None], polarization


def solution(mesh):
    return jax.shard_map(
        body,
        mesh=mesh,
        in_specs=(
            P("energy", None, None, "layer"),
            P(None, None, None, "layer"),
            P(None, None, None, "layer"),
            P(None, "layer"),
            P(),
        ),
        out_specs=(P("energy", None, None, "layer"), P(None, None, ("layer", "energy"))),
        check_vma=False,
    )
```
